32 devices in a mesh: grp: 2 (over x), det: 16 (over z, y, core).
Axes of the slice: x: 2, y: 2, z: 4, core: 2. Of those that a mesh axis runs over, the one named last changes fastest.
Arguments:
- timestream: float32 [2, 1024, 16384], P('grp', 'det'), parts along dimension 0, may hold values from -6 to 6
- gains: float32 [2, 1024], P('grp', 'det'), parts along dimension 0, may hold values from 0.5 to 2
- mode_pattern: float32 [2048, 256], P('grp'), parts along dimension 0, may hold values from -0.375 to 0.375
- mode_weights: float32 [2048, 256], P('grp'), parts along dimension 0, may hold values from -0.1875 to 0.1875
- noise_weight: float32 [2048, 16384], P(('grp', 'det')), parts along dimension 0, may hold values from 0.05 to 1
- block_ids: int32 [2, 1024, 64], P('grp', 'det'), parts along dimension 0, may hold values from 0 to 255
- hits: int32 [2, 1024, 64], P('grp', 'det'), parts along dimension 0, may hold values from 0 to 3
- sky_rows: int32 [512], P('grp'), parts along dimension 0, may hold values from 0 to 255, each once
Outputs:
- filtered: float32 [2, 1024, 16384], P('grp', 'det'), parts along dimension 0
- sky_map: float32 [512, 256], P(('grp', 'det')), parts along dimension 0
The draws below stay inside these ranges and needn't reach their ends.
There are 2 independent parts, one for each index of `grp`. The reference program is written for one: setup_inputs(seed, part) draws one part's arguments, and reference() takes and returns one part's arrays. A program takes and returns all parts, laid end to end along the dimension named above; each array names one. Nothing has to cross between parts.
Inputs may be any that keep to these rules, and one draw needn't show every extreme that they name: `sky_rows`: each row number appears exactly once.
All inputs are finite; a program needn't handle non-finite values.
Results may differ from the reference program's by a relative error of at most 0.000078.
Values sent between devices are 32-bit elements; how exact they have to be, the bound alone decides.
No kernel may reach another device: no remote copies, remote signals or barrier semaphores. Data moves between devices by JAX's collectives and lax.ppermute only.
A program may use at most 128 MiB of HBM per device.

```python
import math
import jax
import jax.numpy as jnp
import numpy as np
from jax import lax

ND = 1024
NS = 16384
RANK = 256
PIX = 256
OBS = 1
NB = 256
NT = 64


def touch_ends(result, own_key, smallest, largest):
    extent = result.shape
    spot = [jax.random.randint(jax.random.fold_in(own_key, axis), (), 0, extent[axis]) for axis in range(len(extent))]
    result = result.at[tuple(spot)].set(smallest)
    longest = extent.index(max(extent))
    spot[longest] = (spot[longest] + 1) % extent[longest]
    return result.at[tuple(spot)].set(largest)


def block_levels(own_key, dims, pieces, low, top_value):
    gain = 1.0
    for axis_at, blocks in pieces:
        draws = jax.random.uniform(jax.random.fold_in(jax.random.fold_in(own_key, 6), axis_at), (blocks,), jnp.float32, low / len(pieces), top_value / len(pieces))
        gain = gain * jnp.repeat(jnp.exp(draws), dims[axis_at] // blocks).reshape((-1,) + (1,) * (len(dims) - 1 - axis_at))
    return gain


def rank_table(number_of, lean):
    loads = [(1 << 20) // math.isqrt(standing ** lean) + 1 for standing in range(1, number_of + 1)]
    deviation = 1 + sum(loads) // (1 << 30)
    return np.cumsum(np.array([max(1, weight // deviation) for weight in loads]))


def skewed_ids(stream_key, extent, count, lean):
    grid = rank_table(count, lean)
    pick = jax.random.randint(jax.random.fold_in(stream_key, 1), extent, 0, int(grid[count - 1]))
    grade = jnp.searchsorted(jnp.asarray(grid, jnp.int32), pick, side="right")
    return jax.random.permutation(jax.random.fold_in(stream_key, 2), count)[grade].astype(jnp.int32)


def gaussian(stream_key, dims, spread, reach, shards=(), held_as=jnp.bfloat16):
    result = spread * jax.random.normal(stream_key, dims, jnp.float32)
    if shards:
        result = result * block_levels(stream_key, dims, shards, -0.22, 0.18)
    return jnp.clip(result, -reach, reach).astype(held_as)


def setup_inputs(seed: int = 0, part: int = 0) -> dict:
    key_list = jax.random.split(jax.random.key(seed), 9)
    part_keys = jax.random.split(jax.random.fold_in(key_list[8], part), 9)
    timestream = gaussian(part_keys[0], (OBS, ND, NS), 1.0, 6.0, ((1, 16),), jnp.float32)
    gains = jnp.clip(jnp.exp(math.log(2.0) - 1.3862944 * jax.random.uniform(part_keys[1], (OBS, ND), jnp.float32) ** block_levels(part_keys[1], (OBS, ND), ((1, 16),), -0.2, 0.2)), 0.5, 2.0)
    mode_pattern = gaussian(part_keys[2], (ND, RANK), RANK ** -0.5, 0.375, (), jnp.float32)
    mode_weights = gaussian(part_keys[3], (ND, RANK), ND ** -0.5, 0.1875, (), jnp.float32)
    noise_weight = jnp.clip(jnp.exp(math.log(1.0) - 2.9957323 * jax.random.uniform(part_keys[4], (ND, NS), jnp.float32) ** block_levels(part_keys[4], (ND, NS), ((0, 16),), -0.2, 0.2)), 0.05, 1.0)
    block_ids = touch_ends(skewed_ids(part_keys[5], (OBS, ND, NT), NB, 2), jax.random.fold_in(part_keys[5], 3), 0, NB - 1).astype(jnp.int32)
    hits = touch_ends(jax.random.randint(part_keys[6], (OBS, ND, NT), 0, 4), jax.random.fold_in(part_keys[6], 1), 0, 3).astype(jnp.int32)
    sky_rows = jax.random.permutation(part_keys[7], NB).astype(jnp.int32)
    return {"timestream": timestream, "gains": gains, "mode_pattern": mode_pattern, "mode_weights": mode_weights, "noise_weight": noise_weight, "block_ids": block_ids, "hits": hits, "sky_rows": sky_rows}


def reference(timestream, gains, mode_pattern, mode_weights, noise_weight, block_ids, hits, sky_rows):
    highest = lax.Precision.HIGHEST
    calibrated = timestream / gains[:, :, None]

    def one_observation(signal):
        coeff = jnp.dot(mode_weights.T, signal, precision=highest, preferred_element_type=jnp.float32)
        corrected = signal - jnp.dot(mode_pattern, coeff, precision=highest, preferred_element_type=jnp.float32)
        spectrum = jnp.fft.fft(corrected, axis=1)
        return jnp.real(jnp.fft.ifft(spectrum * noise_weight, axis=1)).astype(jnp.float32)
    filtered = lax.map(one_observation, calibrated)
    tiles = filtered.reshape(OBS * ND * NT, PIX)
    weight = hits.reshape(-1).astype(jnp.float32)
    rows = sky_rows[block_ids.reshape(-1)]
    sums = jax.ops.segment_sum(tiles * weight[:, None], rows, num_segments=NB)
    counts = jax.ops.segment_sum(weight, rows, num_segments=NB)
    sky_map = sums / jnp.sqrt(1.0 + counts)[:, None]
    return (filtered, sky_map)
```

```python
import functools
import math

import jax
import jax.numpy as jnp
from jax import lax
from jax.experimental import pallas as pl
from jax.experimental.pallas import tpu as pltpu
from jax.sharding import PartitionSpec as P

F32, BF16 = jnp.float32, jnp.bfloat16
ROWS = 8


def halves(value):
    high = value.astype(BF16)
    return high, (value - high.astype(F32)).astype(BF16)


def table_halves(table):
    high = lax.reduce_precision(table, exponent_bits=8, mantissa_bits=7)
    return high.astype(BF16), (table - high).astype(BF16)


def mm(a, b):
    return jnp.dot(a, b, preferred_element_type=F32)


def mm3(a_pair, b_pair):
    return mm(a_pair[0], b_pair[0]) + (mm(a_pair[1], b_pair[0]) + mm(a_pair[0], b_pair[1]))


def angles(count, first, second):
    return (first * second % count).astype(F32) * (2.0 * math.pi / count)


def section_table(side, unit_of_slot):
    unit = unit_of_slot[:, None, None]
    sample = lax.broadcasted_iota(jnp.int32, (1, 1, side), 2)
    part = lax.broadcasted_iota(jnp.int32, (1, 2, 1), 1)
    nyquist = (unit == 0) & (part == 1)
    angle = angles(side, jnp.where(nyquist, side // 2, unit), sample)
    table = jnp.where((part == 0) | nyquist, jnp.cos(angle), -jnp.sin(angle))
    return table.reshape(-1, side)


def inner_tables(side):
    first = lax.broadcasted_iota(jnp.int32, (side, side), 0)
    second = lax.broadcasted_iota(jnp.int32, (side, side), 1)
    angle = angles(side, first, second)
    cos, sin = jnp.cos(angle), jnp.sin(angle)
    forward = jnp.concatenate([jnp.concatenate([cos, -sin], 1), jnp.concatenate([sin, cos], 1)], 0)
    backward = jnp.concatenate([jnp.concatenate([cos, sin], 1), jnp.concatenate([-sin, cos], 1)], 0)
    return forward, backward


def twiddles(side):
    unit = lax.broadcasted_iota(jnp.int32, (side // 2 + 8, side), 0)
    sample = lax.broadcasted_iota(jnp.int32, (side // 2 + 8, side), 1)
    angle = angles(side * side, unit, sample)
    return jnp.cos(angle), jnp.sin(angle)


def section_kernel(side, x_ref, scale_ref, high_ref, low_ref, out_ref, rows, turned):
    scale = scale_ref[...]
    for n in range(side):
        rows[n * ROWS : (n + 1) * ROWS, :] = x_ref[:, n * side : (n + 1) * side] * scale
    table = (high_ref[...], low_ref[...])
    for d in range(0, ROWS, 2):
        pair = jnp.concatenate([rows[pl.ds(d, side, stride=ROWS), :], rows[pl.ds(d + 1, side, stride=ROWS), :]], axis=1)
        result = mm3(table, halves(pair))
        turned[pl.ds(d, side, stride=ROWS), :] = result[:, :side]
        turned[pl.ds(d + 1, side, stride=ROWS), :] = result[:, side:]
    for k in range(side):
        out_ref[k] = turned[k * ROWS : (k + 1) * ROWS, :]


def sections(signal, scale, table):
    dets, samples = signal.shape
    side = table.shape[0]
    high, low = table_halves(table)
    whole = pl.BlockSpec((side, side), lambda i: (0, 0))
    return pl.pallas_call(
        functools.partial(section_kernel, side),
        grid=(dets // ROWS,),
        in_specs=[pl.BlockSpec((ROWS, samples), lambda i: (i, 0)), pl.BlockSpec((ROWS, side), lambda i: (i, 0)), whole, whole],
        out_specs=pl.BlockSpec((side, ROWS, side), lambda i: (0, i, 0)),
        out_shape=jax.ShapeDtypeStruct((side, dets, side), F32),
        scratch_shapes=[pltpu.VMEM((side * ROWS, side), F32), pltpu.VMEM((side * ROWS, side), F32)],
        name="sections",
    )(signal, scale, high, low)


def coeff_kernel(z_ref, high_ref, low_ref, out_ref, z_high, z_low):
    blocks, rows, dets, side = z_ref.shape
    for b in range(blocks):
        for k in range(rows):
            high, low = halves(z_ref[b, k])
            z_high[b * dets : (b + 1) * dets, k * side : (k + 1) * side] = high
            z_low[b * dets : (b + 1) * dets, k * side : (k + 1) * side] = low
    total = mm3((high_ref[...], low_ref[...]), (z_high[...], z_low[...]))
    for k in range(rows):
        out_ref[k] = total[:, k * side : (k + 1) * side]


def coefficients(slab, weights):
    blocks, rows, dets, side = slab.shape
    rank = weights.shape[1]
    high, low = table_halves(weights.T)
    step = 2
    whole = pl.BlockSpec((rank, blocks * dets), lambda i: (0, 0))
    return pl.pallas_call(
        coeff_kernel,
        grid=(rows // step,),
        in_specs=[pl.BlockSpec((blocks, step, dets, side), lambda i: (0, i, 0, 0)), whole, whole],
        out_specs=pl.BlockSpec((step, rank, side), lambda i: (i, 0, 0)),
        out_shape=jax.ShapeDtypeStruct((rows, rank, side), F32),
        scratch_shapes=[pltpu.VMEM((blocks * dets, step * side), BF16)] * 2,
        name="coefficients",
    )(slab, high, low)


def correct_kernel(z_ref, c_ref, high_ref, low_ref, out_ref):
    blocks, rows, dets, side = z_ref.shape
    coeff = halves(jnp.concatenate([c_ref[k] for k in range(rows)], axis=1))
    share = mm3((high_ref[...], low_ref[...]), coeff)
    for b in range(blocks):
        for k in range(rows):
            out_ref[b, k] = z_ref[b, k] - share[b * dets : (b + 1) * dets, k * side : (k + 1) * side]


def corrected(slab, coeff, pattern):
    blocks, rows, dets, side = slab.shape
    rank = pattern.shape[1]
    high, low = table_halves(pattern)
    step = 2
    whole = pl.BlockSpec((blocks * dets, rank), lambda i: (0, 0))
    block = pl.BlockSpec((blocks, step, dets, side), lambda i: (0, i, 0, 0))
    return pl.pallas_call(
        correct_kernel,
        grid=(rows // step,),
        in_specs=[block, pl.BlockSpec((step, rank, side), lambda i: (i, 0, 0)), whole, whole],
        out_specs=block,
        out_shape=jax.ShapeDtypeStruct(slab.shape, F32),
        name="corrected",
    )(slab, coeff, high, low)


def filter_kernel(units, z_ref, w_ref, extra_ref, cos_ref, sin_ref, fh_ref, fl_ref, bh_ref, bl_ref, out_ref, t_high, t_low, result):
    _, dets, side = z_ref.shape
    first = pl.program_id(0) * units
    cos_all = [cos_ref[pl.ds(first + i, 1), :] for i in range(units)]
    sin_all = [sin_ref[pl.ds(first + i, 1), :] for i in range(units)]
    special = (first == 0).astype(F32)
    half_cos, half_sin = cos_ref[pl.ds(side // 2, 1), :], sin_ref[pl.ds(side // 2, 1), :]

    def put(slot, real, imag):
        for part, value in ((0, real), (1, imag)):
            high, low = halves(value)
            t_high[slot * dets : (slot + 1) * dets, part * side : (part + 1) * side] = high
            t_low[slot * dets : (slot + 1) * dets, part * side : (part + 1) * side] = low

    for i in range(units):
        real, imag = z_ref[2 * i], z_ref[2 * i + 1]
        if i == 0:
            put(units, imag * half_cos, -imag * half_sin)
            imag = imag * (1.0 - special)
        put(i, real * cos_all[i] + imag * sin_all[i], imag * cos_all[i] - real * sin_all[i])
    result[...] = mm3((t_high[...], t_low[...]), (fh_ref[...], fl_ref[...]))
    for i in range(units + 1):
        weight = extra_ref[...] if i == units else w_ref[i]
        at = slice(i * dets, (i + 1) * dets)
        put(i, result[at, :side] * weight, result[at, side:] * weight)
    result[...] = mm3((t_high[...], t_low[...]), (bh_ref[...], bl_ref[...]))
    for i in range(units):
        at = slice(i * dets, (i + 1) * dets)
        real, imag = result[at, :side], result[at, side:]
        turned = imag * cos_all[i] + real * sin_all[i]
        if i == 0:
            at = slice(units * dets, (units + 1) * dets)
            nyquist = result[at, :side] * half_cos - result[at, side:] * half_sin
            turned = jnp.where(first == 0, nyquist, turned)
        out_ref[2 * i] = real * cos_all[i] - imag * sin_all[i]
        out_ref[2 * i + 1] = turned


def filter_units(slab, weight, extra):
    rows, dets, side = slab.shape
    units = 8
    forward, backward = inner_tables(side)
    cos, sin = twiddles(side)
    tables = [*table_halves(forward), *table_halves(backward)]
    block = pl.BlockSpec((2 * units, dets, side), lambda i: (i, 0, 0))
    whole = lambda a: pl.BlockSpec(a.shape, lambda i: (0,) * a.ndim)
    return pl.pallas_call(
        functools.partial(filter_kernel, units),
        grid=(rows // (2 * units),),
        in_specs=[block, pl.BlockSpec((units, dets, side), lambda i: (i, 0, 0)), whole(extra), whole(cos), whole(sin)]
        + [whole(t) for t in tables],
        out_specs=block,
        out_shape=jax.ShapeDtypeStruct(slab.shape, F32),
        scratch_shapes=[pltpu.VMEM(((units + 1) * dets, 2 * side), BF16)] * 2 + [pltpu.VMEM(((units + 1) * dets, 2 * side), F32)],
        name="filter_units",
    )(slab, weight, extra, cos, sin, *tables)


def finish_kernel(side, tiles, f_ref, high_ref, low_ref, rows_ref, hits_ref, out_ref, sums_ref, turned, lined, one, t_high, t_low):
    step = pl.program_id(0)
    blocks = sums_ref.shape[0]

    @pl.when(step == 0)
    def _():
        sums_ref[...] = jnp.zeros_like(sums_ref)

    for k in range(side):
        turned[k * ROWS : (k + 1) * ROWS, :] = f_ref[k]
    table = (high_ref[...], low_ref[...])
    for d in range(0, ROWS, 2):
        pair = jnp.concatenate(
            [turned[pl.ds(d, side, stride=ROWS), :], turned[pl.ds(d + 1, side, stride=ROWS), :]], axis=1
        )
        result = mm3(table, halves(pair))
        for e in (0, 1):
            value = result[:, e * side : (e + 1) * side]
            lined[pl.ds(d + e, side, stride=ROWS), :] = value
            one[...] = value
            for half in (0, 1):
                high, low = halves(one[pl.ds(half, side // 2, stride=2), :])
                at = slice((d + e) * tiles, (d + e + 1) * tiles)
                t_high[at, half * side : (half + 1) * side] = high
                t_low[at, half * side : (half + 1) * side] = low
    for n in range(side):
        out_ref[:, n * side : (n + 1) * side] = lined[n * ROWS : (n + 1) * ROWS, :]
    ladder = lax.broadcasted_iota(jnp.int32, (blocks, ROWS * tiles), 0)
    chosen = jnp.where(rows_ref[0] == ladder, hits_ref[0], 0.0).astype(BF16)
    sums_ref[...] += mm(chosen, t_high[...]) + mm(chosen, t_low[...])


def finish(units, table, rows, hits, blocks):
    side, dets, _ = units.shape
    tiles = rows.size // dets
    high, low = table_halves(table)
    whole = pl.BlockSpec((side, side), lambda i: (0, 0))
    line = pl.BlockSpec((1, 1, ROWS * tiles), lambda i: (i, 0, 0))
    steps = dets // ROWS
    return pl.pallas_call(
        functools.partial(finish_kernel, side, tiles),
        grid=(steps,),
        in_specs=[pl.BlockSpec((side, ROWS, side), lambda i: (0, i, 0)), whole, whole, line, line],
        out_specs=[pl.BlockSpec((ROWS, side * side), lambda i: (i, 0)), pl.BlockSpec((blocks, 2 * side), lambda i: (0, 0))],
        out_shape=[jax.ShapeDtypeStruct((dets, side * side), F32), jax.ShapeDtypeStruct((blocks, 2 * side), F32)],
        scratch_shapes=[pltpu.VMEM((side * ROWS, side), F32)] * 2
        + [pltpu.VMEM((side, side), F32)]
        + [pltpu.VMEM((ROWS * tiles, 2 * side), BF16)] * 2,
        name="finish",
    )(units, high, low, rows.reshape(steps, 1, ROWS * tiles), hits.reshape(steps, 1, ROWS * tiles))


def shards(size, timestream, gains, mode_pattern, mode_weights, noise_weight, block_ids, hits, sky_rows):
    _, dets, samples = timestream.shape
    side = math.isqrt(samples)
    units = side // 2
    blocks = sky_rows.shape[0]
    scale = jnp.broadcast_to(1.0 / gains.reshape(dets, 1), (dets, side))
    table = section_table(side, lax.iota(jnp.int32, units))
    z = sections(timestream.reshape(dets, samples), scale, table)

    w = jnp.transpose(noise_weight.reshape(dets, side, side), (2, 0, 1))
    mirror = w[:units:-1, :, ::-1]
    weight = jnp.concatenate([w[:1], w[1:units] + mirror], axis=0)
    extra = w[units]

    slab = lax.all_to_all(z, "det", split_axis=0, concat_axis=0, tiled=True)
    slab = slab.reshape(size, side // size, dets, side)
    coeff = coefficients(slab, mode_weights)
    slab = corrected(slab, coeff, mode_pattern).reshape(side, dets, side)
    z = lax.all_to_all(slab, "det", split_axis=0, concat_axis=0, tiled=True)
    z = filter_units(z, weight, extra)

    ids_flat = block_ids.reshape(-1)
    ladder = lax.broadcasted_iota(jnp.int32, (blocks, ids_flat.shape[0]), 0)
    rows = jnp.sum(jnp.where(ids_flat[None, :] == ladder, sky_rows[:, None], 0), axis=0)
    hit = hits.reshape(-1).astype(F32)
    counts = jnp.sum(jnp.where(rows[None, :] == ladder, hit[None, :], 0.0), axis=1)
    filtered, sums = finish(z, table.T / samples, rows, hit, blocks)

    own = blocks // size
    tail = jnp.pad(counts.reshape(size, 1, own), ((0, 0), (0, ROWS - 1), (0, 2 * side - own)))
    parcel = jnp.concatenate([sums.reshape(size, own, 2 * side), tail], axis=1)
    parcel = lax.all_to_all(parcel, "det", split_axis=0, concat_axis=0, tiled=True)
    parcel = jnp.sum(parcel, axis=0)
    sky_map = parcel[:own] / jnp.sqrt(1.0 + parcel[own, :own])[:, None]
    return filtered.reshape(timestream.shape), sky_map


def solution(mesh):
    in_specs = (
        P("grp", "det", None),
        P("grp", "det"),
        P("grp", None),
        P("grp", None),
        P(("grp", "det"), None),
        P("grp", "det", None),
        P("grp", "det", None),
        P("grp"),
    )
    out_specs = (P("grp", "det", None), P(("grp", "det"), None))
    body = functools.partial(shards, mesh.shape["det"])
    return jax.shard_map(body, mesh=mesh, in_specs=in_specs, out_specs=out_specs, check_vma=False)
```

```python
import functools
import math

import jax
import jax.numpy as jnp
from jax import lax
from jax.experimental import pallas as pl
from jax.experimental.pallas import tpu as pltpu
from jax.sharding import PartitionSpec as P

F32, BF16 = jnp.float32, jnp.bfloat16
ROWS = 8


def halves(value):
    high = value.astype(BF16)
    return high, (value - high.astype(F32)).astype(BF16)


def table_halves(table):
    high = lax.reduce_precision(table, exponent_bits=8, mantissa_bits=7)
    return high.astype(BF16), (table - high).astype(BF16)


def mm(a, b):
    return jnp.dot(a, b, preferred_element_type=F32)


def mm3(a_pair, b_pair):
    return mm(a_pair[0], b_pair[0]) + (mm(a_pair[1], b_pair[0]) + mm(a_pair[0], b_pair[1]))


def angles(count, first, second):
    return (first * second % count).astype(F32) * (2.0 * math.pi / count)


def section_table(side, unit_of_slot):
    unit = unit_of_slot[:, None, None]
    sample = lax.broadcasted_iota(jnp.int32, (1, 1, side), 2)
    part = lax.broadcasted_iota(jnp.int32, (1, 2, 1), 1)
    nyquist = (unit == 0) & (part == 1)
    angle = angles(side, jnp.where(nyquist, side // 2, unit), sample)
    table = jnp.where((part == 0) | nyquist, jnp.cos(angle), -jnp.sin(angle))
    return table.reshape(-1, side)


def inner_tables(side):
    first = lax.broadcasted_iota(jnp.int32, (side, side), 0)
    second = lax.broadcasted_iota(jnp.int32, (side, side), 1)
    angle = angles(side, first, second)
    cos, sin = jnp.cos(angle), jnp.sin(angle)
    forward = jnp.concatenate([jnp.concatenate([cos, -sin], 1), jnp.concatenate([sin, cos], 1)], 0)
    backward = jnp.concatenate([jnp.concatenate([cos, sin], 1), jnp.concatenate([-sin, cos], 1)], 0)
    return forward, backward


def twiddles(side):
    unit = lax.broadcasted_iota(jnp.int32, (side // 2 + 8, side), 0)
    sample = lax.broadcasted_iota(jnp.int32, (side // 2 + 8, side), 1)
    angle = angles(side * side, unit, sample)
    return jnp.cos(angle), jnp.sin(angle)


def section_kernel(side, x_ref, scale_ref, high_ref, low_ref, out_ref, rows, turned):
    scale = scale_ref[...]
    for n in range(side):
        rows[n * ROWS : (n + 1) * ROWS, :] = x_ref[:, n * side : (n + 1) * side] * scale
    table = (high_ref[...], low_ref[...])
    for d in range(0, ROWS, 2):
        pair = jnp.concatenate([rows[pl.ds(d, side, stride=ROWS), :], rows[pl.ds(d + 1, side, stride=ROWS), :]], axis=1)
        result = mm3(table, halves(pair))
        turned[pl.ds(d, side, stride=ROWS), :] = result[:, :side]
        turned[pl.ds(d + 1, side, stride=ROWS), :] = result[:, side:]
    for k in range(side):
        out_ref[k] = turned[k * ROWS : (k + 1) * ROWS, :]


def sections(signal, scale, table):
    dets, samples = signal.shape
    side = table.shape[0]
    high, low = table_halves(table)
    whole = pl.BlockSpec((side, side), lambda i: (0, 0))
    return pl.pallas_call(
        functools.partial(section_kernel, side),
        grid=(dets // ROWS,),
        in_specs=[pl.BlockSpec((ROWS, samples), lambda i: (i, 0)), pl.BlockSpec((ROWS, side), lambda i: (i, 0)), whole, whole],
        out_specs=pl.BlockSpec((side, ROWS, side), lambda i: (0, i, 0)),
        out_shape=jax.ShapeDtypeStruct((side, dets, side), F32),
        scratch_shapes=[pltpu.VMEM((side * ROWS, side), F32), pltpu.VMEM((side * ROWS, side), F32)],
        name="sections",
    )(signal, scale, high, low)


def cost(passes, rows, depth, columns, *arrays):
    moved = sum(array.size * array.dtype.itemsize for array in arrays)
    return pl.CostEstimate(flops=2 * passes * rows * depth * columns, bytes_accessed=moved, transcendentals=0)


def coeff_kernel(near_ref, far_ref, high_ref, low_ref, out_ref, z_high, z_low):
    blocks, rows, dets, side = near_ref.shape
    for b in range(2 * blocks):
        for k in range(rows):
            high, low = halves(near_ref[b, k] if b < blocks else far_ref[b - blocks, k])
            z_high[b * dets : (b + 1) * dets, k * side : (k + 1) * side] = high
            z_low[b * dets : (b + 1) * dets, k * side : (k + 1) * side] = low
    total = mm3((high_ref[...], low_ref[...]), (z_high[...], z_low[...]))
    for k in range(rows):
        out_ref[k] = total[:, k * side : (k + 1) * side]


def coefficients(near, far, weights):
    blocks, rows, dets, side = near.shape
    rank = weights[0].shape[0]
    out = jax.ShapeDtypeStruct((rows, rank, side), F32)
    return pl.pallas_call(
        coeff_kernel,
        out_shape=out,
        scratch_shapes=[pltpu.VMEM((2 * blocks * dets, rows * side), BF16)] * 2,
        cost_estimate=cost(3, rank, 2 * blocks * dets, rows * side, near, far, out),
        name="coefficients",
    )(near, far, *weights)


def correct_kernel(terms, near_ref, far_ref, *refs):
    c_refs, (high_ref, low_ref, near_out, far_out) = refs[:terms], refs[terms:]
    blocks, rows, dets, side = near_ref.shape
    coeff = halves(jnp.concatenate([sum(c_ref[k] for c_ref in c_refs) for k in range(rows)], axis=1))
    share = mm3((high_ref[...], low_ref[...]), coeff)
    for b in range(2 * blocks):
        source, target, at = (near_ref, near_out, b) if b < blocks else (far_ref, far_out, b - blocks)
        for k in range(rows):
            target[at, k] = source[at, k] - share[b * dets : (b + 1) * dets, k * side : (k + 1) * side]


def corrected(near, far, coeffs, pattern):
    blocks, rows, dets, side = near.shape
    rank = pattern[0].shape[1]
    out = jax.ShapeDtypeStruct(near.shape, F32)
    return pl.pallas_call(
        functools.partial(correct_kernel, len(coeffs)),
        out_shape=[out, out],
        cost_estimate=cost(3, rank, 2 * blocks * dets, rows * side, near, far, out, out, *coeffs),
        name="corrected",
    )(near, far, *coeffs, *pattern)


def filter_kernel(chunk, pieces, me_ref, *refs):
    z_refs, refs = refs[:pieces], refs[pieces:]
    w_ref, extra_ref, cos_ref, sin_ref, fh_ref, fl_ref, bh_ref, bl_ref, out_ref, t_high, t_low, result = refs
    rows, dets, side = z_refs[0].shape
    units = rows // 2
    me = me_ref[0]
    has_zero = chunk == 0
    count = pieces * units
    half_cos, half_sin = cos_ref[pl.ds(side // 2, 1), :], sin_ref[pl.ds(side // 2, 1), :]

    def turn(slot):
        unit = (chunk * pieces + (me ^ (slot // units))) * units + slot % units
        return cos_ref[pl.ds(unit, 1), :], sin_ref[pl.ds(unit, 1), :]

    def put(slot, real, imag):
        for part, value in ((0, real), (1, imag)):
            high, low = halves(value)
            t_high[slot * dets : (slot + 1) * dets, part * side : (part + 1) * side] = high
            t_low[slot * dets : (slot + 1) * dets, part * side : (part + 1) * side] = low

    folded = jnp.zeros((dets, side), F32)
    for slot in range(count):
        piece, unit = divmod(slot, units)
        real, imag = z_refs[piece][2 * unit], z_refs[piece][2 * unit + 1]
        if has_zero and unit == 0:
            folded = jnp.where(me == piece, imag, folded)
            imag = jnp.where(me == piece, 0.0, imag)
        cos, sin = turn(slot)
        put(slot, real * cos + imag * sin, imag * cos - real * sin)
    if has_zero:
        put(count, folded * half_cos, -folded * half_sin)
    result[...] = mm3((t_high[...], t_low[...]), (fh_ref[...], fl_ref[...]))
    for slot in range(count + has_zero):
        weight = extra_ref[...] if slot == count else w_ref[me ^ (slot // units), slot % units]
        at = slice(slot * dets, (slot + 1) * dets)
        put(slot, result[at, :side] * weight, result[at, side:] * weight)
    result[...] = mm3((t_high[...], t_low[...]), (bh_ref[...], bl_ref[...]))
    if has_zero:
        at = slice(count * dets, (count + 1) * dets)
        folded = result[at, :side] * half_cos - result[at, side:] * half_sin
    for slot in range(count):
        at = slice(slot * dets, (slot + 1) * dets)
        real, imag = result[at, :side], result[at, side:]
        cos, sin = turn(slot)
        turned = imag * cos + real * sin
        if has_zero and slot % units == 0:
            turned = jnp.where(me == slot // units, folded, turned)
        out_ref[2 * slot] = real * cos - imag * sin
        out_ref[2 * slot + 1] = turned


def filter_units(chunk, me, pieces, weight, extra, tables):
    rows, dets, side = pieces[0].shape
    count = len(pieces) * rows // 2
    out = jax.ShapeDtypeStruct((2 * count, dets, side), F32)
    held = (count + (chunk == 0)) * dets
    vmem = pl.BlockSpec(memory_space=pltpu.VMEM)
    share = pl.BlockSpec((None,) + weight.shape[1:], lambda i: (chunk, 0, 0, 0, 0))
    whole = lambda a: pl.BlockSpec(a.shape, lambda i: (0,) * a.ndim)
    return pl.pallas_call(
        functools.partial(filter_kernel, chunk, len(pieces)),
        grid=(1,),
        in_specs=[pl.BlockSpec(memory_space=pltpu.SMEM)] + [whole(p) for p in pieces] + [share, whole(extra)] + [whole(t) for t in tables],
        out_specs=pl.BlockSpec(out.shape, lambda i: (0, 0, 0)),
        out_shape=out,
        scratch_shapes=[pltpu.VMEM((held, 2 * side), BF16)] * 2 + [pltpu.VMEM((held, 2 * side), F32)],
        cost_estimate=cost(6, held, 2 * side, 2 * side, out, out, out),
        name="filter_units",
    )(me, *pieces, weight, extra, *tables)


def finish_kernel(side, tiles, chunks, *refs):
    f_refs, refs = refs[:chunks], refs[chunks:]
    high_ref, low_ref, rows_ref, hits_ref, out_ref, sums_ref, turned, lined, one, t_high, t_low = refs
    step = pl.program_id(0)
    blocks = sums_ref.shape[0]

    @pl.when(step == 0)
    def _():
        sums_ref[...] = jnp.zeros_like(sums_ref)

    for k in range(side):
        chunk, row = divmod(k, side // chunks)
        turned[k * ROWS : (k + 1) * ROWS, :] = f_refs[chunk][row]
    table = (high_ref[...], low_ref[...])
    for d in range(0, ROWS, 2):
        pair = jnp.concatenate(
            [turned[pl.ds(d, side, stride=ROWS), :], turned[pl.ds(d + 1, side, stride=ROWS), :]], axis=1
        )
        result = mm3(table, halves(pair))
        for e in (0, 1):
            value = result[:, e * side : (e + 1) * side]
            lined[pl.ds(d + e, side, stride=ROWS), :] = value
            one[...] = value
            for half in (0, 1):
                high, low = halves(one[pl.ds(half, side // 2, stride=2), :])
                at = slice((d + e) * tiles, (d + e + 1) * tiles)
                t_high[at, half * side : (half + 1) * side] = high
                t_low[at, half * side : (half + 1) * side] = low
    for n in range(side):
        out_ref[:, n * side : (n + 1) * side] = lined[n * ROWS : (n + 1) * ROWS, :]
    ladder = lax.broadcasted_iota(jnp.int32, (blocks, ROWS * tiles), 0)
    chosen = jnp.where(rows_ref[0] == ladder, hits_ref[0], 0.0).astype(BF16)
    sums_ref[...] += mm(chosen, t_high[...]) + mm(chosen, t_low[...])


def finish(units, table, rows, hits, blocks):
    _, dets, side = units[0].shape
    tiles = rows.size // dets
    high, low = table_halves(table)
    whole = pl.BlockSpec((side, side), lambda i: (0, 0))
    line = pl.BlockSpec((1, 1, ROWS * tiles), lambda i: (i, 0, 0))
    steps = dets // ROWS
    return pl.pallas_call(
        functools.partial(finish_kernel, side, tiles, len(units)),
        grid=(steps,),
        in_specs=[pl.BlockSpec((u.shape[0], ROWS, side), lambda i: (0, i, 0)) for u in units] + [whole, whole, line, line],
        out_specs=[pl.BlockSpec((ROWS, side * side), lambda i: (i, 0)), pl.BlockSpec((blocks, 2 * side), lambda i: (0, 0))],
        out_shape=[jax.ShapeDtypeStruct((dets, side * side), F32), jax.ShapeDtypeStruct((blocks, 2 * side), F32)],
        scratch_shapes=[pltpu.VMEM((side * ROWS, side), F32)] * 2
        + [pltpu.VMEM((side, side), F32)]
        + [pltpu.VMEM((ROWS * tiles, 2 * side), BF16)] * 2,
        name="finish",
    )(*units, high, low, rows.reshape(steps, 1, ROWS * tiles), hits.reshape(steps, 1, ROWS * tiles))


class Planes:
    def __init__(self, size):
        self.width = 1 << ((size.bit_length() - 1) // 2)
        self.count = size // self.width
        pairs = [(2 * i, 2 * i + 1) if i % 2 == 0 else (2 * i + 1, 2 * i) for i in range(self.count // 2)]
        self.outer = [pair[0] for pair in pairs]
        self.worker = [pair[1] for pair in pairs]

    def send(self, value, routes):
        pairs = [(a * self.width + q, b * self.width + (q ^ k)) for a, b, k in routes for q in range(self.width)]
        return lax.ppermute(value, "det", pairs)

    def swap(self, value, k):
        return self.send(value, [(p, p, k) for p in range(self.count)])

    def inward(self, value):
        return self.send(value, [(a, b, 0) for a, b in zip(self.outer, self.worker)])

    def outward(self, value):
        return self.send(value, [(b, a, 0) for a, b in zip(self.outer, self.worker)])

    def others(self, value):
        count = len(self.worker)
        turns = [[(self.worker[i], self.worker[(i + t) % count], 0) for i in range(count)] for t in range(1, count)]
        return [self.send(value, turn) for turn in turns]


CHUNKS = 8


def shards(size, timestream, gains, mode_pattern, mode_weights, noise_weight, block_ids, hits, sky_rows):
    _, dets, samples = timestream.shape
    side = math.isqrt(samples)
    units = side // 2
    blocks = sky_rows.shape[0]
    planes = Planes(size)
    width = planes.width
    share = units // (CHUNKS * width)
    index = lax.axis_index("det")
    plane, me = index // width, index % width
    outer = jnp.zeros((), bool)
    partner = jnp.zeros((), jnp.int32)
    for a, b in zip(planes.outer, planes.worker):
        outer = outer | (plane == a)
        partner = jnp.where(plane == a, b, jnp.where(plane == b, a, partner))

    scale = jnp.broadcast_to(1.0 / gains.reshape(dets, 1), (dets, side))
    slot = lax.iota(jnp.int32, units)
    chunk, piece, item = slot // (width * share), slot // share % width, slot % share
    table = section_table(side, (chunk * width + (piece ^ me)) * share + item)
    z = sections(timestream.reshape(dets, samples), scale, table)
    z = z.reshape(CHUNKS, width, 2 * share, dets, side)

    order = jnp.concatenate([p * width + (lax.iota(jnp.int32, width) ^ me) for p in (plane, partner)])

    def ordered(modes):
        modes = modes.reshape(size, dets, -1)
        parts = [lax.dynamic_index_in_dim(modes, order[i], 0, keepdims=False) for i in range(2 * width)]
        return jnp.concatenate(parts, axis=0)

    weights = table_halves(ordered(mode_weights).T)
    pattern = table_halves(ordered(mode_pattern))
    w = jnp.transpose(noise_weight.reshape(dets, side, side), (2, 0, 1))
    mirror = w[:units:-1, :, ::-1]
    weight = jnp.concatenate([w[:1], w[1:units] + mirror], axis=0).reshape(CHUNKS, width, share, dets, side)
    extra = w[units]
    forward, backward = inner_tables(side)
    tables = [*twiddles(side), *table_halves(forward), *table_halves(backward)]

    done = []
    for c in range(CHUNKS):
        near = jnp.stack([z[c, 0]] + [planes.swap(z[c, k], k) for k in range(1, width)])
        far = planes.inward(near)
        coeff = coefficients(near, far, weights)
        near, far = corrected(near, far, [coeff] + planes.others(coeff), pattern)
        back = jnp.where(outer, planes.outward(far), near)
        pieces = [back[0]] + [planes.swap(back[k], k) for k in range(1, width)]
        done.append(filter_units(c, me.reshape(1), pieces, weight, extra, tables))

    ids_flat = block_ids.reshape(-1)
    ladder = lax.broadcasted_iota(jnp.int32, (blocks, ids_flat.shape[0]), 0)
    rows = jnp.sum(jnp.where(ids_flat[None, :] == ladder, sky_rows[:, None], 0), axis=0)
    hit = hits.reshape(-1).astype(F32)
    counts = jnp.sum(jnp.where(rows[None, :] == ladder, hit[None, :], 0.0), axis=1)
    filtered, sums = finish(done, table.T / samples, rows, hit, blocks)

    own = blocks // size
    tail = jnp.pad(counts.reshape(size, 1, own), ((0, 0), (0, ROWS - 1), (0, 2 * side - own)))
    parcel = jnp.concatenate([sums.reshape(size, own, 2 * side), tail], axis=1)
    parcel = lax.all_to_all(parcel, "det", split_axis=0, concat_axis=0, tiled=True)
    parcel = jnp.sum(parcel, axis=0)
    sky_map = parcel[:own] / jnp.sqrt(1.0 + parcel[own, :own])[:, None]
    return filtered.reshape(timestream.shape), sky_map


def solution(mesh):
    in_specs = (
        P("grp", "det", None),
        P("grp", "det"),
        P("grp", None),
        P("grp", None),
        P(("grp", "det"), None),
        P("grp", "det", None),
        P("grp", "det", None),
        P("grp"),
    )
    out_specs = (P("grp", "det", None), P(("grp", "det"), None))
    body = functools.partial(shards, mesh.shape["det"])
    return jax.shard_map(body, mesh=mesh, in_specs=in_specs, out_specs=out_specs, check_vma=False)
```

```python
import functools
import math

import jax
import jax.numpy as jnp
from jax import lax
from jax.experimental import pallas as pl
from jax.experimental.pallas import tpu as pltpu
from jax.sharding import PartitionSpec as P


F32, BF16 = jnp.float32, jnp.bfloat16
ROWS = 8
UNITS = 8
PARTS = (1, 1)
LIMIT = pltpu.CompilerParams(vmem_limit_bytes=16 << 20)


def halves(value):
    high = value.astype(BF16)
    return high, (value - high.astype(F32)).astype(BF16)


def table_halves(table):
    high = lax.reduce_precision(table, exponent_bits=8, mantissa_bits=7)
    return high.astype(BF16), (table - high).astype(BF16)


def mm(a, b):
    return jnp.dot(a, b, preferred_element_type=F32)


def mm3(a_pair, b_pair):
    return mm(a_pair[0], b_pair[0]) + (mm(a_pair[1], b_pair[0]) + mm(a_pair[0], b_pair[1]))


def angles(count, first, second):
    return (first * second % count).astype(F32) * (2.0 * math.pi / count)


def section_table(side, unit_of_slot):
    unit = unit_of_slot[:, None, None]
    sample = lax.broadcasted_iota(jnp.int32, (1, 1, side), 2)
    part = lax.broadcasted_iota(jnp.int32, (1, 2, 1), 1)
    nyquist = (unit == 0) & (part == 1)
    angle = angles(side, jnp.where(nyquist, side // 2, unit), sample)
    table = jnp.where((part == 0) | nyquist, jnp.cos(angle), -jnp.sin(angle))
    return table.reshape(-1, side)


def inner_tables(side):
    first = lax.broadcasted_iota(jnp.int32, (side, side), 0)
    second = lax.broadcasted_iota(jnp.int32, (side, side), 1)
    angle = angles(side, first, second)
    cos, sin = jnp.cos(angle), jnp.sin(angle)
    forward = jnp.concatenate([jnp.concatenate([cos, -sin], 1), jnp.concatenate([sin, cos], 1)], 0)
    backward = jnp.concatenate([jnp.concatenate([cos, sin], 1), jnp.concatenate([-sin, cos], 1)], 0)
    return forward, backward


def twiddles(side):
    unit = lax.broadcasted_iota(jnp.int32, (side // 2 + 8, side), 0)
    sample = lax.broadcasted_iota(jnp.int32, (side // 2 + 8, side), 1)
    angle = angles(side * side, unit, sample)
    return jnp.cos(angle), jnp.sin(angle)


def section_kernel(side, x_ref, scale_ref, high_ref, low_ref, *refs):
    out_refs, (rows, turned) = refs[:-2], refs[-2:]
    scale = scale_ref[...]
    for n in range(side):
        rows[n * ROWS : (n + 1) * ROWS, :] = x_ref[:, n * side : (n + 1) * side] * scale
    table = (high_ref[...], low_ref[...])
    for d in range(0, ROWS, 2):
        pair = jnp.concatenate([rows[pl.ds(d, side, stride=ROWS), :], rows[pl.ds(d + 1, side, stride=ROWS), :]], axis=1)
        result = mm3(table, halves(pair))
        turned[pl.ds(d, side, stride=ROWS), :] = result[:, :side]
        turned[pl.ds(d + 1, side, stride=ROWS), :] = result[:, side:]
    lines = [(out_ref, row) for out_ref in out_refs for row in range(out_ref.shape[0])]
    for k, (out_ref, row) in enumerate(lines):
        out_ref[row] = turned[k * ROWS : (k + 1) * ROWS, :]


def sections(signal, scale, table, shares):
    dets, samples = signal.shape
    side = table.shape[0]
    high, low = table_halves(table)
    whole = pl.BlockSpec((side, side), lambda i: (0, 0))
    return pl.pallas_call(
        functools.partial(section_kernel, side),
        grid=(dets // ROWS,),
        in_specs=[pl.BlockSpec((ROWS, samples), lambda i: (i, 0)), pl.BlockSpec((ROWS, side), lambda i: (i, 0)), whole, whole],
        out_specs=[pl.BlockSpec((share, ROWS, side), lambda i: (0, i, 0)) for share in shares],
        out_shape=[jax.ShapeDtypeStruct((share, dets, side), F32) for share in shares],
        scratch_shapes=[pltpu.VMEM((side * ROWS, side), F32), pltpu.VMEM((side * ROWS, side), F32)],
        compiler_params=LIMIT,
        name="sections",
    )(signal, scale, high, low)


def cost(passes, rows, depth, columns, *arrays):
    moved = sum(array.size * array.dtype.itemsize for array in arrays)
    return pl.CostEstimate(flops=2 * passes * rows * depth * columns, bytes_accessed=moved, transcendentals=0)


def coeff_kernel(z_ref, high_ref, low_ref, out_ref, z_high, z_low):
    blocks, rows, dets, side = z_ref.shape
    for b in range(blocks):
        for k in range(rows):
            high, low = halves(z_ref[b, k])
            z_high[b * dets : (b + 1) * dets, k * side : (k + 1) * side] = high
            z_low[b * dets : (b + 1) * dets, k * side : (k + 1) * side] = low
    total = mm3((high_ref[...], low_ref[...]), (z_high[...], z_low[...]))
    for k in range(rows):
        out_ref[k] = total[:, k * side : (k + 1) * side]


def coefficients(slab, weights):
    blocks, rows, dets, side = slab.shape
    rank = weights[0].shape[0]
    out = jax.ShapeDtypeStruct((rows, rank, side), F32)
    step = math.gcd(2, rows)
    whole = pl.BlockSpec((rank, blocks * dets), lambda i: (0, 0))
    return pl.pallas_call(
        coeff_kernel,
        grid=(rows // step,),
        in_specs=[pl.BlockSpec((blocks, step, dets, side), lambda i: (0, i, 0, 0)), whole, whole],
        out_specs=pl.BlockSpec((step, rank, side), lambda i: (i, 0, 0)),
        out_shape=out,
        scratch_shapes=[pltpu.VMEM((blocks * dets, step * side), BF16)] * 2,
        compiler_params=LIMIT,
        cost_estimate=cost(3, rank, blocks * dets, rows * side, slab, out),
        name="coefficients",
    )(slab, *weights)


def correct_kernel(terms, z_ref, *refs):
    c_refs, (high_ref, low_ref, out_ref) = refs[:terms], refs[terms:]
    blocks, rows, dets, side = z_ref.shape
    coeff = halves(jnp.concatenate([sum(c_ref[k] for c_ref in c_refs) for k in range(rows)], axis=1))
    share = mm3((high_ref[...], low_ref[...]), coeff)
    for b in range(blocks):
        for k in range(rows):
            out_ref[b, k] = z_ref[b, k] - share[b * dets : (b + 1) * dets, k * side : (k + 1) * side]


def corrected(slab, coeffs, pattern):
    blocks, rows, dets, side = slab.shape
    rank = pattern[0].shape[1]
    step = math.gcd(2, rows)
    whole = pl.BlockSpec((blocks * dets, rank), lambda i: (0, 0))
    block = pl.BlockSpec((blocks, step, dets, side), lambda i: (0, i, 0, 0))
    return pl.pallas_call(
        functools.partial(correct_kernel, len(coeffs)),
        grid=(rows // step,),
        in_specs=[block] + [pl.BlockSpec((step, rank, side), lambda i: (i, 0, 0)) for _ in coeffs] + [whole, whole],
        out_specs=block,
        out_shape=jax.ShapeDtypeStruct(slab.shape, F32),
        compiler_params=LIMIT,
        cost_estimate=cost(3, rank, blocks * dets, rows * side, slab, slab, *coeffs),
        name="corrected",
    )(slab, *coeffs, *pattern)


def filter_kernel(base, count, z_ref, w_ref, extra_ref, cos_ref, sin_ref, fh_ref, fl_ref, bh_ref, bl_ref, out_ref, t_high, t_low, result):
    _, dets, side = z_ref.shape
    step = pl.program_id(0)
    first = base + step * count
    half_cos, half_sin = cos_ref[pl.ds(side // 2, 1), :], sin_ref[pl.ds(side // 2, 1), :]
    turns = [(cos_ref[pl.ds(first + i, 1), :], sin_ref[pl.ds(first + i, 1), :]) for i in range(count)]
    has_zero = base == 0

    def put(slot, real, imag):
        for part, value in ((0, real), (1, imag)):
            high, low = halves(value)
            t_high[slot * dets : (slot + 1) * dets, part * side : (part + 1) * side] = high
            t_low[slot * dets : (slot + 1) * dets, part * side : (part + 1) * side] = low

    for i in range(count):
        real, imag = z_ref[2 * i], z_ref[2 * i + 1]
        if has_zero and i == 0:
            put(count, imag * half_cos, -imag * half_sin)
            imag = jnp.where(first == 0, 0.0, imag)
        cos, sin = turns[i]
        put(i, real * cos + imag * sin, imag * cos - real * sin)
    result[...] = mm3((t_high[...], t_low[...]), (fh_ref[...], fl_ref[...]))
    for i in range(count + has_zero):
        weight = extra_ref[...] if i == count else w_ref[i]
        at = slice(i * dets, (i + 1) * dets)
        put(i, result[at, :side] * weight, result[at, side:] * weight)
    result[...] = mm3((t_high[...], t_low[...]), (bh_ref[...], bl_ref[...]))
    for i in range(count):
        at = slice(i * dets, (i + 1) * dets)
        real, imag = result[at, :side], result[at, side:]
        cos, sin = turns[i]
        turned = imag * cos + real * sin
        if has_zero and i == 0:
            at = slice(count * dets, (count + 1) * dets)
            nyquist = result[at, :side] * half_cos - result[at, side:] * half_sin
            turned = jnp.where(first == 0, nyquist, turned)
        out_ref[2 * i] = real * cos - imag * sin
        out_ref[2 * i + 1] = turned


def filter_units(base, slab, weight, extra, tables):
    rows, dets, side = slab.shape
    count = math.gcd(math.gcd(rows // 2, UNITS), base) if base else math.gcd(rows // 2, UNITS)
    held = (count + (base == 0)) * dets
    whole = lambda a: pl.BlockSpec(a.shape, lambda i: (0,) * a.ndim)
    block = pl.BlockSpec((2 * count, dets, side), lambda i: (i, 0, 0))
    return pl.pallas_call(
        functools.partial(filter_kernel, base, count),
        grid=(rows // (2 * count),),
        in_specs=[block, pl.BlockSpec((count, dets, side), lambda i: (base // count + i, 0, 0)), whole(extra)]
        + [whole(t) for t in tables],
        out_specs=block,
        out_shape=jax.ShapeDtypeStruct(slab.shape, F32),
        scratch_shapes=[pltpu.VMEM((held, 2 * side), BF16)] * 2 + [pltpu.VMEM((held, 2 * side), F32)],
        compiler_params=LIMIT,
        cost_estimate=cost(6, rows // 2 * dets, 2 * side, 2 * side, slab, slab, slab),
        name="filter_units",
    )(slab, weight, extra, *tables)


def finish_kernel(side, tiles, chunks, *refs):
    f_refs, refs = refs[:chunks], refs[chunks:]
    high_ref, low_ref, rows_ref, hits_ref, out_ref, sums_ref, turned, lined, one, t_high, t_low = refs
    step = pl.program_id(0)
    blocks = sums_ref.shape[0]

    @pl.when(step == 0)
    def _():
        sums_ref[...] = jnp.zeros_like(sums_ref)

    lines = [f_ref[row] for f_ref in f_refs for row in range(f_ref.shape[0])]
    for k in range(side):
        turned[k * ROWS : (k + 1) * ROWS, :] = lines[k]
    table = (high_ref[...], low_ref[...])
    for d in range(0, ROWS, 2):
        pair = jnp.concatenate(
            [turned[pl.ds(d, side, stride=ROWS), :], turned[pl.ds(d + 1, side, stride=ROWS), :]], axis=1
        )
        result = mm3(table, halves(pair))
        for e in (0, 1):
            value = result[:, e * side : (e + 1) * side]
            lined[pl.ds(d + e, side, stride=ROWS), :] = value
            one[...] = value
            for half in (0, 1):
                high, low = halves(one[pl.ds(half, side // 2, stride=2), :])
                at = slice((d + e) * tiles, (d + e + 1) * tiles)
                t_high[at, half * side : (half + 1) * side] = high
                t_low[at, half * side : (half + 1) * side] = low
    for n in range(side):
        out_ref[:, n * side : (n + 1) * side] = lined[n * ROWS : (n + 1) * ROWS, :]
    ladder = lax.broadcasted_iota(jnp.int32, (blocks, ROWS * tiles), 0)
    chosen = jnp.where(rows_ref[0] == ladder, hits_ref[0], 0.0).astype(BF16)
    sums_ref[...] += mm(chosen, t_high[...]) + mm(chosen, t_low[...])


def finish(units, table, rows, hits, blocks):
    _, dets, side = units[0].shape
    tiles = rows.size // dets
    high, low = table_halves(table)
    whole = pl.BlockSpec((side, side), lambda i: (0, 0))
    line = pl.BlockSpec((1, 1, ROWS * tiles), lambda i: (i, 0, 0))
    steps = dets // ROWS
    return pl.pallas_call(
        functools.partial(finish_kernel, side, tiles, len(units)),
        grid=(steps,),
        in_specs=[pl.BlockSpec((u.shape[0], ROWS, side), lambda i: (0, i, 0)) for u in units] + [whole, whole, line, line],
        out_specs=[pl.BlockSpec((ROWS, side * side), lambda i: (i, 0)), pl.BlockSpec((blocks, 2 * side), lambda i: (0, 0))],
        out_shape=[jax.ShapeDtypeStruct((dets, side * side), F32), jax.ShapeDtypeStruct((blocks, 2 * side), F32)],
        scratch_shapes=[pltpu.VMEM((side * ROWS, side), F32)] * 2
        + [pltpu.VMEM((side, side), F32)]
        + [pltpu.VMEM((ROWS * tiles, 2 * side), BF16)] * 2,
        compiler_params=LIMIT,
        name="finish",
    )(*units, high, low, rows.reshape(steps, 1, ROWS * tiles), hits.reshape(steps, 1, ROWS * tiles))


def shards(size, timestream, gains, mode_pattern, mode_weights, noise_weight, block_ids, hits, sky_rows):
    _, dets, samples = timestream.shape
    side = math.isqrt(samples)
    units = side // 2
    blocks = sky_rows.shape[0]
    half = size // 2
    groups = [list(range(half)), list(range(half, size))]
    opposite = [(i, (i + half) % size) for i in range(size)]
    mine = lax.axis_index("det") // half

    starts = [side * sum(PARTS[:c]) // sum(PARTS) for c in range(len(PARTS) + 1)]
    shares = [b - a for a, b in zip(starts, starts[1:])]
    chunks = range(len(PARTS))

    scale = jnp.broadcast_to(1.0 / gains.reshape(dets, 1), (dets, side))
    table = section_table(side, lax.iota(jnp.int32, units))
    z = sections(timestream.reshape(dets, samples), scale, table, shares)

    def of_half(modes):
        return lax.dynamic_index_in_dim(modes.reshape(2, half * dets, -1), mine, 0, keepdims=False)

    weights = table_halves(of_half(mode_weights).T)
    pattern = table_halves(of_half(mode_pattern))
    w = jnp.transpose(noise_weight.reshape(dets, side, side), (2, 0, 1))
    mirror = w[:units:-1, :, ::-1]
    weight = jnp.concatenate([w[:1], w[1:units] + mirror], axis=0)
    extra = w[units]
    forward, backward = inner_tables(side)
    tables = [*twiddles(side), *table_halves(forward), *table_halves(backward)]

    last = [None]

    def exchange(value):
        if last[0] is not None:
            value, _ = lax.optimization_barrier((value, last[0]))
        last[0] = lax.all_to_all(value, "det", split_axis=0, concat_axis=0, axis_index_groups=groups, tiled=True)
        return last[0]

    slabs, coeffs, others = [], [], []
    for c in chunks:
        slabs.append(exchange(z[c]).reshape(half, shares[c] // half, dets, side))
        coeffs.append(coefficients(slabs[c], weights))
        last[0] = coeffs[c]
        others.append(lax.ppermute(coeffs[c], "det", opposite))
    done = []
    for c in chunks:
        slab = corrected(slabs[c], [coeffs[c], others[c]], pattern)
        back = exchange(slab.reshape(shares[c], dets, side))
        done.append(filter_units(starts[c] // 2, back, weight, extra, tables))

    ids_flat = block_ids.reshape(-1)
    ladder = lax.broadcasted_iota(jnp.int32, (blocks, ids_flat.shape[0]), 0)
    rows = jnp.sum(jnp.where(ids_flat[None, :] == ladder, sky_rows[:, None], 0), axis=0)
    hit = hits.reshape(-1).astype(F32)
    counts = jnp.sum(jnp.where(rows[None, :] == ladder, hit[None, :], 0.0), axis=1)
    filtered, sums = finish(done, table.T / samples, rows, hit, blocks)

    own = blocks // size
    tail = jnp.pad(counts.reshape(size, 1, own), ((0, 0), (0, ROWS - 1), (0, 2 * side - own)))
    parcel = jnp.concatenate([sums.reshape(size, own, 2 * side), tail], axis=1)
    parcel = lax.all_to_all(parcel, "det", split_axis=0, concat_axis=0, tiled=True)
    parcel = jnp.sum(parcel, axis=0)
    sky_map = parcel[:own] / jnp.sqrt(1.0 + parcel[own, :own])[:, None]
    return filtered.reshape(timestream.shape), sky_map


def solution(mesh):
    in_specs = (
        P("grp", "det", None),
        P("grp", "det"),
        P("grp", None),
        P("grp", None),
        P(("grp", "det"), None),
        P("grp", "det", None),
        P("grp", "det", None),
        P("grp"),
    )
    out_specs = (P("grp", "det", None), P(("grp", "det"), None))
    body = functools.partial(shards, mesh.shape["det"])

    return jax.shard_map(body, mesh=mesh, in_specs=in_specs, out_specs=out_specs, check_vma=False)
```

```python
import functools
import math

import jax
import jax.numpy as jnp
from jax import lax
from jax.experimental import pallas as pl
from jax.experimental.pallas import tpu as pltpu
from jax.sharding import PartitionSpec as P


F32, BF16 = jnp.float32, jnp.bfloat16
ROWS = 8
UNITS = 8
PARTS = (1, 1)
LIMIT = pltpu.CompilerParams(vmem_limit_bytes=16 << 20)


def halves(value):
    high = value.astype(BF16)
    return high, (value - high.astype(F32)).astype(BF16)


def table_halves(table):
    high = lax.reduce_precision(table, exponent_bits=8, mantissa_bits=7)
    return high.astype(BF16), (table - high).astype(BF16)


def mm(a, b):
    return jnp.dot(a, b, preferred_element_type=F32)


def mm3(a_pair, b_pair):
    return mm(a_pair[0], b_pair[0]) + (mm(a_pair[1], b_pair[0]) + mm(a_pair[0], b_pair[1]))


def angles(count, first, second):
    return (first * second % count).astype(F32) * (2.0 * math.pi / count)


def section_table(side, unit_of_slot):
    unit = unit_of_slot[:, None, None]
    sample = lax.broadcasted_iota(jnp.int32, (1, 1, side), 2)
    part = lax.broadcasted_iota(jnp.int32, (1, 2, 1), 1)
    nyquist = (unit == 0) & (part == 1)
    angle = angles(side, jnp.where(nyquist, side // 2, unit), sample)
    table = jnp.where((part == 0) | nyquist, jnp.cos(angle), -jnp.sin(angle))
    return table.reshape(-1, side)


def inner_tables(side):
    first = lax.broadcasted_iota(jnp.int32, (side, side), 0)
    second = lax.broadcasted_iota(jnp.int32, (side, side), 1)
    angle = angles(side, first, second)
    cos, sin = jnp.cos(angle), jnp.sin(angle)
    forward = jnp.concatenate([jnp.concatenate([cos, -sin], 1), jnp.concatenate([sin, cos], 1)], 0)
    backward = jnp.concatenate([jnp.concatenate([cos, sin], 1), jnp.concatenate([-sin, cos], 1)], 0)
    return forward, backward


def twiddles(side):
    unit = lax.broadcasted_iota(jnp.int32, (side // 2 + 8, side), 0)
    sample = lax.broadcasted_iota(jnp.int32, (side // 2 + 8, side), 1)
    angle = angles(side * side, unit, sample)
    return jnp.cos(angle), jnp.sin(angle)


def section_kernel(side, x_ref, scale_ref, high_ref, low_ref, *refs):
    out_refs, (rows, turned) = refs[:-2], refs[-2:]
    scale = scale_ref[...]
    for n in range(side):
        rows[n * ROWS : (n + 1) * ROWS, :] = x_ref[:, n * side : (n + 1) * side] * scale
    table = (high_ref[...], low_ref[...])
    for d in range(0, ROWS, 2):
        pair = jnp.concatenate([rows[pl.ds(d, side, stride=ROWS), :], rows[pl.ds(d + 1, side, stride=ROWS), :]], axis=1)
        result = mm3(table, halves(pair))
        turned[pl.ds(d, side, stride=ROWS), :] = result[:, :side]
        turned[pl.ds(d + 1, side, stride=ROWS), :] = result[:, side:]
    lines = [(out_ref, row) for out_ref in out_refs for row in range(out_ref.shape[0])]
    for k, (out_ref, row) in enumerate(lines):
        out_ref[row] = turned[k * ROWS : (k + 1) * ROWS, :]


def sections(signal, scale, table, shares):
    dets, samples = signal.shape
    side = table.shape[0]
    high, low = table_halves(table)
    whole = pl.BlockSpec((side, side), lambda i: (0, 0))
    return pl.pallas_call(
        functools.partial(section_kernel, side),
        grid=(dets // ROWS,),
        in_specs=[pl.BlockSpec((ROWS, samples), lambda i: (i, 0)), pl.BlockSpec((ROWS, side), lambda i: (i, 0)), whole, whole],
        out_specs=[pl.BlockSpec((share, ROWS, side), lambda i: (0, i, 0)) for share in shares],
        out_shape=[jax.ShapeDtypeStruct((share, dets, side), F32) for share in shares],
        scratch_shapes=[pltpu.VMEM((side * ROWS, side), F32), pltpu.VMEM((side * ROWS, side), F32)],
        compiler_params=LIMIT,
        name="sections",
    )(signal, scale, high, low)


def cost(passes, rows, depth, columns, *arrays):
    moved = sum(array.size * array.dtype.itemsize for array in arrays)
    return pl.CostEstimate(flops=2 * passes * rows * depth * columns, bytes_accessed=moved, transcendentals=0)


def coeff_kernel(z_ref, high_ref, low_ref, out_ref, z_high, z_low):
    blocks, rows, dets, side = z_ref.shape
    for b in range(blocks):
        for k in range(rows):
            high, low = halves(z_ref[b, k])
            z_high[b * dets : (b + 1) * dets, k * side : (k + 1) * side] = high
            z_low[b * dets : (b + 1) * dets, k * side : (k + 1) * side] = low
    total = mm3((high_ref[...], low_ref[...]), (z_high[...], z_low[...]))
    for k in range(rows):
        out_ref[k] = total[:, k * side : (k + 1) * side]


def coefficients(slab, weights):
    blocks, rows, dets, side = slab.shape
    rank = weights[0].shape[0]
    out = jax.ShapeDtypeStruct((rows, rank, side), F32)
    step = math.gcd(2, rows)
    whole = pl.BlockSpec((rank, blocks * dets), lambda i: (0, 0))
    return pl.pallas_call(
        coeff_kernel,
        grid=(rows // step,),
        in_specs=[pl.BlockSpec((blocks, step, dets, side), lambda i: (0, i, 0, 0)), whole, whole],
        out_specs=pl.BlockSpec((step, rank, side), lambda i: (i, 0, 0)),
        out_shape=out,
        scratch_shapes=[pltpu.VMEM((blocks * dets, step * side), BF16)] * 2,
        compiler_params=LIMIT,
        cost_estimate=cost(3, rank, blocks * dets, rows * side, slab, out),
        name="coefficients",
    )(slab, *weights)


def correct_kernel(terms, z_ref, *refs):
    c_refs, (high_ref, low_ref, out_ref) = refs[:terms], refs[terms:]
    blocks, rows, dets, side = z_ref.shape
    coeff = halves(jnp.concatenate([sum(c_ref[k] for c_ref in c_refs) for k in range(rows)], axis=1))
    share = mm3((high_ref[...], low_ref[...]), coeff)
    for b in range(blocks):
        for k in range(rows):
            out_ref[b, k] = z_ref[b, k] - share[b * dets : (b + 1) * dets, k * side : (k + 1) * side]


def corrected(slab, coeffs, pattern):
    blocks, rows, dets, side = slab.shape
    rank = pattern[0].shape[1]
    step = math.gcd(2, rows)
    whole = pl.BlockSpec((blocks * dets, rank), lambda i: (0, 0))
    block = pl.BlockSpec((blocks, step, dets, side), lambda i: (0, i, 0, 0))
    return pl.pallas_call(
        functools.partial(correct_kernel, len(coeffs)),
        grid=(rows // step,),
        in_specs=[block] + [pl.BlockSpec((step, rank, side), lambda i: (i, 0, 0)) for _ in coeffs] + [whole, whole],
        out_specs=block,
        out_shape=jax.ShapeDtypeStruct(slab.shape, F32),
        compiler_params=LIMIT,
        cost_estimate=cost(3, rank, blocks * dets, rows * side, slab, slab, *coeffs),
        name="corrected",
    )(slab, *coeffs, *pattern)


def filter_kernel(base, count, z_ref, w_ref, extra_ref, cos_ref, sin_ref, fh_ref, fl_ref, bh_ref, bl_ref, out_ref, t_high, t_low, result):
    _, dets, side = z_ref.shape
    step = pl.program_id(0)
    first = base + step * count
    half_cos, half_sin = cos_ref[pl.ds(side // 2, 1), :], sin_ref[pl.ds(side // 2, 1), :]
    turns = [(cos_ref[pl.ds(first + i, 1), :], sin_ref[pl.ds(first + i, 1), :]) for i in range(count)]
    has_zero = base == 0

    def put(slot, real, imag):
        for part, value in ((0, real), (1, imag)):
            high, low = halves(value)
            t_high[slot * dets : (slot + 1) * dets, part * side : (part + 1) * side] = high
            t_low[slot * dets : (slot + 1) * dets, part * side : (part + 1) * side] = low

    for i in range(count):
        real, imag = z_ref[2 * i], z_ref[2 * i + 1]
        if has_zero and i == 0:
            put(count, imag * half_cos, -imag * half_sin)
            imag = jnp.where(first == 0, 0.0, imag)
        cos, sin = turns[i]
        put(i, real * cos + imag * sin, imag * cos - real * sin)
    result[...] = mm3((t_high[...], t_low[...]), (fh_ref[...], fl_ref[...]))
    for i in range(count + has_zero):
        weight = extra_ref[...] if i == count else w_ref[i]
        at = slice(i * dets, (i + 1) * dets)
        put(i, result[at, :side] * weight, result[at, side:] * weight)
    result[...] = mm3((t_high[...], t_low[...]), (bh_ref[...], bl_ref[...]))
    for i in range(count):
        at = slice(i * dets, (i + 1) * dets)
        real, imag = result[at, :side], result[at, side:]
        cos, sin = turns[i]
        turned = imag * cos + real * sin
        if has_zero and i == 0:
            at = slice(count * dets, (count + 1) * dets)
            nyquist = result[at, :side] * half_cos - result[at, side:] * half_sin
            turned = jnp.where(first == 0, nyquist, turned)
        out_ref[2 * i] = real * cos - imag * sin
        out_ref[2 * i + 1] = turned


def filter_units(base, slab, weight, extra, tables):
    rows, dets, side = slab.shape
    count = math.gcd(math.gcd(rows // 2, UNITS), base) if base else math.gcd(rows // 2, UNITS)
    held = (count + (base == 0)) * dets
    whole = lambda a: pl.BlockSpec(a.shape, lambda i: (0,) * a.ndim)
    block = pl.BlockSpec((2 * count, dets, side), lambda i: (i, 0, 0))
    return pl.pallas_call(
        functools.partial(filter_kernel, base, count),
        grid=(rows // (2 * count),),
        in_specs=[block, pl.BlockSpec((count, dets, side), lambda i: (base // count + i, 0, 0)), whole(extra)]
        + [whole(t) for t in tables],
        out_specs=block,
        out_shape=jax.ShapeDtypeStruct(slab.shape, F32),
        scratch_shapes=[pltpu.VMEM((held, 2 * side), BF16)] * 2 + [pltpu.VMEM((held, 2 * side), F32)],
        compiler_params=LIMIT,
        cost_estimate=cost(6, rows // 2 * dets, 2 * side, 2 * side, slab, slab, slab),
        name="filter_units",
    )(slab, weight, extra, *tables)


def finish_kernel(side, tiles, chunks, *refs):
    f_refs, refs = refs[:chunks], refs[chunks:]
    high_ref, low_ref, rows_ref, hits_ref, out_ref, sums_ref, turned, lined, one, t_high, t_low = refs
    step = pl.program_id(0)
    blocks = sums_ref.shape[0]

    @pl.when(step == 0)
    def _():
        sums_ref[...] = jnp.zeros_like(sums_ref)

    lines = [f_ref[row] for f_ref in f_refs for row in range(f_ref.shape[0])]
    for k in range(side):
        turned[k * ROWS : (k + 1) * ROWS, :] = lines[k]
    table = (high_ref[...], low_ref[...])
    for d in range(0, ROWS, 2):
        pair = jnp.concatenate(
            [turned[pl.ds(d, side, stride=ROWS), :], turned[pl.ds(d + 1, side, stride=ROWS), :]], axis=1
        )
        result = mm3(table, halves(pair))
        for e in (0, 1):
            value = result[:, e * side : (e + 1) * side]
            lined[pl.ds(d + e, side, stride=ROWS), :] = value
            one[...] = value
            for half in (0, 1):
                high, low = halves(one[pl.ds(half, side // 2, stride=2), :])
                at = slice((d + e) * tiles, (d + e + 1) * tiles)
                t_high[at, half * side : (half + 1) * side] = high
                t_low[at, half * side : (half + 1) * side] = low
    for n in range(side):
        out_ref[:, n * side : (n + 1) * side] = lined[n * ROWS : (n + 1) * ROWS, :]
    ladder = lax.broadcasted_iota(jnp.int32, (blocks, ROWS * tiles), 0)
    chosen = jnp.where(rows_ref[0] == ladder, hits_ref[0], 0.0).astype(BF16)
    sums_ref[...] += mm(chosen, t_high[...]) + mm(chosen, t_low[...])


def finish(units, table, rows, hits, blocks):
    _, dets, side = units[0].shape
    tiles = rows.size // dets
    high, low = table_halves(table)
    whole = pl.BlockSpec((side, side), lambda i: (0, 0))
    line = pl.BlockSpec((1, 1, ROWS * tiles), lambda i: (i, 0, 0))
    steps = dets // ROWS
    return pl.pallas_call(
        functools.partial(finish_kernel, side, tiles, len(units)),
        grid=(steps,),
        in_specs=[pl.BlockSpec((u.shape[0], ROWS, side), lambda i: (0, i, 0)) for u in units] + [whole, whole, line, line],
        out_specs=[pl.BlockSpec((ROWS, side * side), lambda i: (i, 0)), pl.BlockSpec((blocks, 2 * side), lambda i: (0, 0))],
        out_shape=[jax.ShapeDtypeStruct((dets, side * side), F32), jax.ShapeDtypeStruct((blocks, 2 * side), F32)],
        scratch_shapes=[pltpu.VMEM((side * ROWS, side), F32)] * 2
        + [pltpu.VMEM((side, side), F32)]
        + [pltpu.VMEM((ROWS * tiles, 2 * side), BF16)] * 2,
        compiler_params=LIMIT,
        name="finish",
    )(*units, high, low, rows.reshape(steps, 1, ROWS * tiles), hits.reshape(steps, 1, ROWS * tiles))


def shards(size, timestream, gains, mode_pattern, mode_weights, noise_weight, block_ids, hits, sky_rows):
    _, dets, samples = timestream.shape
    side = math.isqrt(samples)
    units = side // 2
    blocks = sky_rows.shape[0]
    half = size // 2
    quarter = size // 4
    groups = [list(range(half)), [*range(half + quarter, size), *range(half, half + quarter)]]
    opposite = [*zip(groups[0], groups[1]), *zip(groups[1], groups[0])]
    mine = lax.axis_index("det") // half

    starts = [side * sum(PARTS[:c]) // sum(PARTS) for c in range(len(PARTS) + 1)]
    shares = [b - a for a, b in zip(starts, starts[1:])]
    chunks = range(len(PARTS))

    scale = jnp.broadcast_to(1.0 / gains.reshape(dets, 1), (dets, side))
    table = section_table(side, lax.iota(jnp.int32, units))
    z = sections(timestream.reshape(dets, samples), scale, table, shares)

    def of_half(modes):
        modes = modes.reshape(4, quarter * dets, -1)
        parts = [lax.dynamic_index_in_dim(modes, at, 0, keepdims=False) for at in (3 * mine, 1 + mine)]
        return jnp.concatenate(parts, axis=0)

    weights = table_halves(of_half(mode_weights).T)
    pattern = table_halves(of_half(mode_pattern))
    w = jnp.transpose(noise_weight.reshape(dets, side, side), (2, 0, 1))
    mirror = w[:units:-1, :, ::-1]
    weight = jnp.concatenate([w[:1], w[1:units] + mirror], axis=0)
    extra = w[units]
    forward, backward = inner_tables(side)
    tables = [*twiddles(side), *table_halves(forward), *table_halves(backward)]

    last = [None]

    def exchange(value):
        if last[0] is not None:
            value, _ = lax.optimization_barrier((value, last[0]))
        last[0] = lax.all_to_all(value, "det", split_axis=0, concat_axis=0, axis_index_groups=groups, tiled=True)
        return last[0]

    slabs, coeffs, others = [], [], []
    for c in chunks:
        slabs.append(exchange(z[c]).reshape(half, shares[c] // half, dets, side))
        coeffs.append(coefficients(slabs[c], weights))
        others.append(lax.ppermute(coeffs[c], "det", opposite))
    done = []
    for c in chunks:
        slab = corrected(slabs[c], [coeffs[c], others[c]], pattern)
        back = exchange(slab.reshape(shares[c], dets, side))
        done.append(filter_units(starts[c] // 2, back, weight, extra, tables))

    ids_flat = block_ids.reshape(-1)
    ladder = lax.broadcasted_iota(jnp.int32, (blocks, ids_flat.shape[0]), 0)
    rows = jnp.sum(jnp.where(ids_flat[None, :] == ladder, sky_rows[:, None], 0), axis=0)
    hit = hits.reshape(-1).astype(F32)
    counts = jnp.sum(jnp.where(rows[None, :] == ladder, hit[None, :], 0.0), axis=1)
    filtered, sums = finish(done, table.T / samples, rows, hit, blocks)

    own = blocks // size
    tail = jnp.pad(counts.reshape(size, 1, own), ((0, 0), (0, ROWS - 1), (0, 2 * side - own)))
    parcel = jnp.concatenate([sums.reshape(size, own, 2 * side), tail], axis=1)
    parcel = lax.all_to_all(parcel, "det", split_axis=0, concat_axis=0, tiled=True)
    parcel = jnp.sum(parcel, axis=0)
    sky_map = parcel[:own] / jnp.sqrt(1.0 + parcel[own, :own])[:, None]
    return filtered.reshape(timestream.shape), sky_map


def solution(mesh):
    in_specs = (
        P("grp", "det", None),
        P("grp", "det"),
        P("grp", None),
        P("grp", None),
        P(("grp", "det"), None),
        P("grp", "det", None),
        P("grp", "det", None),
        P("grp"),
    )
    out_specs = (P("grp", "det", None), P(("grp", "det"), None))
    body = functools.partial(shards, mesh.shape["det"])

    return jax.shard_map(body, mesh=mesh, in_specs=in_specs, out_specs=out_specs, check_vma=False)
```

```python
import functools
import math

import jax
import jax.numpy as jnp
from jax import lax
from jax.experimental import pallas as pl
from jax.experimental.pallas import tpu as pltpu
from jax.sharding import PartitionSpec as P


F32, BF16 = jnp.float32, jnp.bfloat16
ROWS = 8
UNITS = 8
LIMIT = pltpu.CompilerParams(vmem_limit_bytes=16 << 20)


def halves(value):
    high = value.astype(BF16)
    return high, (value - high.astype(F32)).astype(BF16)


def table_halves(table):
    high = lax.reduce_precision(table, exponent_bits=8, mantissa_bits=7)
    return high.astype(BF16), (table - high).astype(BF16)


def mm(a, b):
    return jnp.dot(a, b, preferred_element_type=F32)


def mm3(a_pair, b_pair):
    return mm(a_pair[0], b_pair[0]) + (mm(a_pair[1], b_pair[0]) + mm(a_pair[0], b_pair[1]))


def angles(count, first, second):
    return (first * second % count).astype(F32) * (2.0 * math.pi / count)


def section_table(side, unit_of_slot):
    unit = unit_of_slot[:, None, None]
    sample = lax.broadcasted_iota(jnp.int32, (1, 1, side), 2)
    part = lax.broadcasted_iota(jnp.int32, (1, 2, 1), 1)
    nyquist = (unit == 0) & (part == 1)
    angle = angles(side, jnp.where(nyquist, side // 2, unit), sample)
    table = jnp.where((part == 0) | nyquist, jnp.cos(angle), -jnp.sin(angle))
    return table.reshape(-1, side)


def inner_tables(side):
    first = lax.broadcasted_iota(jnp.int32, (side, side), 0)
    second = lax.broadcasted_iota(jnp.int32, (side, side), 1)
    angle = angles(side, first, second)
    cos, sin = jnp.cos(angle), jnp.sin(angle)
    forward = jnp.concatenate([jnp.concatenate([cos, -sin], 1), jnp.concatenate([sin, cos], 1)], 0)
    backward = jnp.concatenate([jnp.concatenate([cos, sin], 1), jnp.concatenate([-sin, cos], 1)], 0)
    return forward, backward


def twiddles(side):
    unit = lax.broadcasted_iota(jnp.int32, (side // 2 + 8, side), 0)
    sample = lax.broadcasted_iota(jnp.int32, (side // 2 + 8, side), 1)
    angle = angles(side * side, unit, sample)
    return jnp.cos(angle), jnp.sin(angle)


def section_kernel(side, x_ref, scale_ref, high_ref, low_ref, *refs):
    out_refs, (rows, turned) = refs[:-2], refs[-2:]
    scale = scale_ref[...]
    for n in range(side):
        rows[n * ROWS : (n + 1) * ROWS, :] = x_ref[:, n * side : (n + 1) * side] * scale
    table = (high_ref[...], low_ref[...])
    for d in range(0, ROWS, 2):
        pair = jnp.concatenate([rows[pl.ds(d, side, stride=ROWS), :], rows[pl.ds(d + 1, side, stride=ROWS), :]], axis=1)
        result = mm3(table, halves(pair))
        turned[pl.ds(d, len(result), stride=ROWS), :] = result[:, :side]
        turned[pl.ds(d + 1, len(result), stride=ROWS), :] = result[:, side:]
    lines = [(out_ref, row) for out_ref in out_refs for row in range(out_ref.shape[0])]
    for k, (out_ref, row) in enumerate(lines):
        out_ref[row] = turned[k * ROWS : (k + 1) * ROWS, :]


def sections(signal, scale, table, shares):
    dets, samples = signal.shape
    side = table.shape[1]
    high, low = table_halves(table)
    whole = pl.BlockSpec(table.shape, lambda i: (0, 0))
    return pl.pallas_call(
        functools.partial(section_kernel, side),
        grid=(dets // ROWS,),
        in_specs=[pl.BlockSpec((ROWS, samples), lambda i: (i, 0)), pl.BlockSpec((ROWS, side), lambda i: (i, 0)), whole, whole],
        out_specs=[pl.BlockSpec((share, ROWS, side), lambda i: (0, i, 0)) for share in shares],
        out_shape=[jax.ShapeDtypeStruct((share, dets, side), F32) for share in shares],
        scratch_shapes=[pltpu.VMEM((side * ROWS, side), F32), pltpu.VMEM((sum(shares) * ROWS, side), F32)],
        compiler_params=LIMIT,
        name="sections",
    )(signal, scale, high, low)


def cost(passes, rows, depth, columns, *arrays):
    moved = sum(array.size * array.dtype.itemsize for array in arrays)
    return pl.CostEstimate(flops=2 * passes * rows * depth * columns, bytes_accessed=moved, transcendentals=0)


def coeff_kernel(z_ref, high_ref, low_ref, out_ref, z_high, z_low):
    blocks, rows, dets, side = z_ref.shape
    for b in range(blocks):
        for k in range(rows):
            high, low = halves(z_ref[b, k])
            z_high[b * dets : (b + 1) * dets, k * side : (k + 1) * side] = high
            z_low[b * dets : (b + 1) * dets, k * side : (k + 1) * side] = low
    total = mm3((high_ref[...], low_ref[...]), (z_high[...], z_low[...]))
    for k in range(rows):
        out_ref[k] = total[:, k * side : (k + 1) * side]


def coefficients(slab, weights):
    blocks, rows, dets, side = slab.shape
    rank = weights[0].shape[0]
    out = jax.ShapeDtypeStruct((rows, rank, side), F32)
    step = math.gcd(2, rows)
    whole = pl.BlockSpec((rank, blocks * dets), lambda i: (0, 0))
    return pl.pallas_call(
        coeff_kernel,
        grid=(rows // step,),
        in_specs=[pl.BlockSpec((blocks, step, dets, side), lambda i: (0, i, 0, 0)), whole, whole],
        out_specs=pl.BlockSpec((step, rank, side), lambda i: (i, 0, 0)),
        out_shape=out,
        scratch_shapes=[pltpu.VMEM((blocks * dets, step * side), BF16)] * 2,
        compiler_params=LIMIT,
        cost_estimate=cost(3, rank, blocks * dets, rows * side, slab, out),
        name="coefficients",
    )(slab, *weights)


def correct_kernel(terms, z_ref, *refs):
    c_refs, (high_ref, low_ref, out_ref) = refs[:terms], refs[terms:]
    blocks, rows, dets, side = z_ref.shape
    coeff = halves(jnp.concatenate([sum(c_ref[k] for c_ref in c_refs) for k in range(rows)], axis=1))
    share = mm3((high_ref[...], low_ref[...]), coeff)
    for b in range(blocks):
        for k in range(rows):
            out_ref[b, k] = z_ref[b, k] - share[b * dets : (b + 1) * dets, k * side : (k + 1) * side]


def corrected(slab, coeffs, pattern):
    blocks, rows, dets, side = slab.shape
    rank = pattern[0].shape[1]
    step = math.gcd(2, rows)
    whole = pl.BlockSpec((blocks * dets, rank), lambda i: (0, 0))
    block = pl.BlockSpec((blocks, step, dets, side), lambda i: (0, i, 0, 0))
    return pl.pallas_call(
        functools.partial(correct_kernel, len(coeffs)),
        grid=(rows // step,),
        in_specs=[block] + [pl.BlockSpec((step, rank, side), lambda i: (i, 0, 0)) for _ in coeffs] + [whole, whole],
        out_specs=block,
        out_shape=jax.ShapeDtypeStruct(slab.shape, F32),
        compiler_params=LIMIT,
        cost_estimate=cost(3, rank, blocks * dets, rows * side, slab, slab, *coeffs),
        name="corrected",
    )(slab, *coeffs, *pattern)


def section_lines(group, section_ref, d, rows):
    pair = [group[pl.ds(d + e, rows, stride=ROWS), :] for e in (0, 1)]
    high, low = halves(jnp.concatenate(pair, axis=1))
    return mm(section_ref[...], jnp.concatenate([high, low, high], axis=0))


def synth_kernel(base, count, steps, z_ref, w_ref, extra_ref, turn_ref, tables_ref, section_ref, rows_ref, hits_ref, *refs):
    *ends, t_high, t_low, result, held, tile_high, tile_low, total_ref, one = refs
    ending = len(ends) == 4
    _, dets, side = z_ref.shape
    step = pl.program_id(0)

    @pl.when(step < steps)
    def _():
        first = base + step * count
        has_zero = base == 0

        def turn(unit):
            pair = turn_ref[pl.ds(unit, 1), :]
            return pair[:, :side], pair[:, side:]

        half_cos, half_sin = turn(side // 2)
        turns = [turn(first + i) for i in range(count)]
        table = lambda i: tables_ref[i * 2 * side : (i + 1) * 2 * side, :]

        def put(slot, real, imag):
            for part, value in ((0, real), (1, imag)):
                high, low = halves(value)
                t_high[slot * dets : (slot + 1) * dets, part * side : (part + 1) * side] = high
                t_low[slot * dets : (slot + 1) * dets, part * side : (part + 1) * side] = low

        def transform(high, low):
            middle = result.shape[0] // 2 // 16 * 16
            for at in (slice(0, middle), slice(middle, result.shape[0])):
                result[at] = mm3((t_high[at], t_low[at]), (table(high), table(low)))

        for i in range(count):
            real, imag = z_ref[2 * i], z_ref[2 * i + 1]
            if has_zero and i == 0:
                put(count, imag * half_cos, -imag * half_sin)
                imag = jnp.where(first == 0, 0.0, imag)
            cos, sin = turns[i]
            put(i, real * cos + imag * sin, imag * cos - real * sin)
        transform(0, 1)
        for i in range(count + has_zero):
            weight = extra_ref[...] if i == count else w_ref[i]
            at = slice(i * dets, (i + 1) * dets)
            put(i, result[at, :side] * weight, result[at, side:] * weight)
        transform(2, 3)
        for i in range(count):
            at = slice(i * dets, (i + 1) * dets)
            real, imag = result[at, :side], result[at, side:]
            cos, sin = turns[i]
            turned = imag * cos + real * sin
            if has_zero and i == 0:
                at = slice(count * dets, (count + 1) * dets)
                nyquist = result[at, :side] * half_cos - result[at, side:] * half_sin
                turned = jnp.where(first == 0, nyquist, turned)
            for part, value in ((0, real * cos - imag * sin), (1, turned)):
                row = pl.multiple_of((2 * (step * count + i) + part) * ROWS, ROWS)
                for group in range(dets // ROWS):
                    held[group, pl.ds(row, ROWS), :] = value[group * ROWS : (group + 1) * ROWS]

    @pl.when(step >= steps)
    def _():
        rows = 2 * count * steps
        tiles = tile_high.shape[0] // ROWS
        group = held.at[step - steps]
        lines_ref = one if ending else ends[0]
        for d in range(0, ROWS, 2):
            lines = section_lines(group, section_ref, d, rows)
            for e in (0, 1):
                at = (d + e) * side
                lines_ref[at : at + side, :] = lines[:, e * side : (e + 1) * side]
                for half in (0, 1):
                    high, low = halves(lines_ref[pl.ds(at + half, side // 2, stride=2), :])
                    into = slice((d + e) * tiles, (d + e + 1) * tiles)
                    tile_high[into, half * side : (half + 1) * side] = high
                    tile_low[into, half * side : (half + 1) * side] = low
        if ending:
            ends[2][0] = group[...]
        sums_ref = total_ref if ending else ends[1]
        ladder = lax.broadcasted_iota(jnp.int32, (sums_ref.shape[0], ROWS * tiles), 0)
        chosen = jnp.where(rows_ref[0] == ladder, hits_ref[0], 0.0).astype(BF16)
        total = mm(chosen, tile_high[...]) + mm(chosen, tile_low[...])
        before = ends[0][...] if ending else 0.0
        sums_ref[...] = total + jnp.where(step == steps, before, sums_ref[...])
        if ending:
            _, tail_ref, _, parcel_ref = ends

            @pl.when(step == pl.num_programs(0) - 1)
            def _():
                own = sums_ref.shape[0] // parcel_ref.shape[0]
                for owner in range(parcel_ref.shape[0]):
                    parcel_ref[owner, :own] = sums_ref[owner * own : (owner + 1) * own, :]
                    parcel_ref[owner, own:] = tail_ref[owner]


def stacked(section):
    high, low = table_halves(section)
    return jnp.concatenate([high, high, low], axis=1)


def synth(base, slab, weight, extra, turns, tables, section, rows, hits, blocks, ending=()):
    lines, dets, side = slab.shape
    tiles = rows.size // dets
    count = math.gcd(lines // 2, UNITS)
    steps, groups = lines // (2 * count), dets // ROWS
    room = (count + (base == 0)) * dets
    whole = lambda a: pl.BlockSpec(a.shape, lambda i: (0,) * a.ndim)
    later = lambda i: jnp.maximum(i - steps, 0)
    line = pl.BlockSpec((1, 1, ROWS * tiles), lambda i: (later(i), 0, 0))
    operands = [slab, weight, extra, turns, tables, section, rows.reshape(groups, 1, -1), hits.reshape(groups, 1, -1), *ending]
    in_specs = [
        pl.BlockSpec((2 * count, dets, side), lambda i: (jnp.minimum(i, steps - 1), 0, 0)),
        pl.BlockSpec((count, dets, side), lambda i: (base // count + jnp.minimum(i, steps - 1), 0, 0)),
        *[whole(a) for a in operands[2:6]],
        line,
        line,
        *[whole(a) for a in ending],
    ]
    if ending:
        _, tail = ending
        parcel = (tail.shape[0], blocks // tail.shape[0] + tail.shape[1], tail.shape[2])
        out = [jax.ShapeDtypeStruct((groups, lines * ROWS, side), F32), jax.ShapeDtypeStruct(parcel, F32)]
        out_specs = [pl.BlockSpec((1, lines * ROWS, side), lambda i: (later(i), 0, 0)), whole(out[1])]
    else:
        out = [jax.ShapeDtypeStruct((dets * side, side), F32), jax.ShapeDtypeStruct((blocks, 2 * side), F32)]
        out_specs = [pl.BlockSpec((ROWS * side, side), lambda i: (later(i), 0)), whole(out[1])]
    return pl.pallas_call(
        functools.partial(synth_kernel, base, count, steps),
        grid=(steps + groups,),
        in_specs=in_specs,
        out_specs=out_specs,
        out_shape=out,
        scratch_shapes=[
            *[pltpu.VMEM((room, 2 * side), BF16)] * 2,
            pltpu.VMEM((room, 2 * side), F32),
            pltpu.VMEM((groups, lines * ROWS, side), F32),
            *[pltpu.VMEM((ROWS * tiles, 2 * side), BF16)] * 2,
            pltpu.VMEM((blocks, 2 * side), F32),
            pltpu.VMEM((ROWS * side, side), F32),
        ],
        compiler_params=LIMIT,
        cost_estimate=cost(8, lines // 2 * dets, 2 * side, 2 * side, slab, slab, out[0]),
        name="synth",
    )(*operands)


def emit_kernel(before_ref, held_ref, section_ref, out_ref, lined):
    side = before_ref.shape[1]
    rows = held_ref.shape[1] // ROWS
    for d in range(0, ROWS, 2):
        lines = section_lines(held_ref.at[0], section_ref, d, rows)
        for e in (0, 1):
            at = (d + e) * side
            line = lines[:, e * side : (e + 1) * side] + before_ref[at : at + side, :]
            lined[pl.ds(d + e, side, stride=ROWS), :] = line
    for n in range(side):
        out_ref[:, n * side : (n + 1) * side] = lined[n * ROWS : (n + 1) * ROWS, :]


def emit(before, held, section):
    groups, lines, side = held.shape
    out = jax.ShapeDtypeStruct((groups * ROWS, side * side), F32)
    return pl.pallas_call(
        emit_kernel,
        grid=(groups,),
        in_specs=[
            pl.BlockSpec((ROWS * side, side), lambda i: (i, 0)),
            pl.BlockSpec((1, lines, side), lambda i: (i, 0, 0)),
            pl.BlockSpec(section.shape, lambda i: (0, 0)),
        ],
        out_specs=pl.BlockSpec((ROWS, side * side), lambda i: (i, 0)),
        out_shape=out,
        scratch_shapes=[pltpu.VMEM((ROWS * side, side), F32)],
        compiler_params=LIMIT,
        cost_estimate=cost(1, side, lines // ROWS, ROWS * groups * side, before, held, out),
        name="emit",
    )(before, held, section)


def shards(size, timestream, gains, mode_pattern, mode_weights, noise_weight, block_ids, hits, sky_rows):
    _, dets, samples = timestream.shape
    side = math.isqrt(samples)
    units = side // 2
    blocks = sky_rows.shape[0]
    half = size // 2
    quarter = size // 4
    groups = [list(range(half)), [*range(half + quarter, size), *range(half, half + quarter)]]
    opposite = [*zip(groups[0], groups[1]), *zip(groups[1], groups[0])]
    mine = lax.axis_index("det") // half

    scale = jnp.broadcast_to(1.0 / gains.reshape(dets, 1), (dets, side))
    table = section_table(side, lax.iota(jnp.int32, units))
    share = side // 2
    parts = [table[:share], table[share:]]
    stacks = [stacked(part.T / samples) for part in parts]
    z = []
    for part in parts:
        z += sections(timestream.reshape(dets, samples), scale, part, [share])

    def of_half(modes):
        modes = modes.reshape(4, quarter * dets, -1)
        parts = [lax.dynamic_index_in_dim(modes, at, 0, keepdims=False) for at in (3 * mine, 1 + mine)]
        return jnp.concatenate(parts, axis=0)

    weights = table_halves(of_half(mode_weights).T)
    pattern = table_halves(of_half(mode_pattern))
    w = jnp.transpose(noise_weight.reshape(dets, side, side), (2, 0, 1))
    mirror = w[:units:-1, :, ::-1]
    weight = jnp.concatenate([w[:1], w[1:units] + mirror], axis=0)
    extra = w[units]
    forward, backward = inner_tables(side)
    tables = jnp.concatenate([*table_halves(forward), *table_halves(backward)], axis=0)
    turns = jnp.concatenate(twiddles(side), axis=1)

    ids_flat = block_ids.reshape(-1)
    ladder = lax.broadcasted_iota(jnp.int32, (blocks, ids_flat.shape[0]), 0)
    rows = jnp.sum(jnp.where(ids_flat[None, :] == ladder, sky_rows[:, None], 0), axis=0)
    hit = hits.reshape(-1).astype(F32)
    counts = jnp.sum(jnp.where(rows[None, :] == ladder, hit[None, :], 0.0), axis=1)

    own = blocks // size
    tail = jnp.pad(counts.reshape(size, 1, own), ((0, 0), (0, ROWS - 1), (0, 2 * side - own)))

    last = [None]

    def exchange(value):
        if last[0] is not None:
            value, _ = lax.optimization_barrier((value, last[0]))
        last[0] = lax.all_to_all(value, "det", split_axis=0, concat_axis=0, axis_index_groups=groups, tiled=True)
        return last[0]

    slabs, coeffs, others = [], [], []
    for c in (0, 1):
        slabs.append(exchange(z[c]).reshape(half, share // half, dets, side))
        coeffs.append(coefficients(slabs[c], weights))
        others.append(lax.ppermute(coeffs[c], "det", opposite))
    for c in (0, 1):
        slab = corrected(slabs[c], [coeffs[c], others[c]], pattern)
        back = exchange(slab.reshape(share, dets, side))
        operands = [c * units // 2, back, weight, extra, turns, tables, stacks[c], rows, hit, blocks]
        if c == 0:
            lines, sums = synth(*operands)
        else:
            held, parcel = synth(*operands, ending=(sums, tail))

    parcel = lax.all_to_all(parcel, "det", split_axis=0, concat_axis=0, tiled=True)
    filtered = emit(lines, held, stacks[1])
    parcel = jnp.sum(parcel, axis=0)
    sky_map = parcel[:own] / jnp.sqrt(1.0 + parcel[own, :own])[:, None]
    return filtered.reshape(timestream.shape), sky_map


def solution(mesh):
    in_specs = (
        P("grp", "det", None),
        P("grp", "det"),
        P("grp", None),
        P("grp", None),
        P(("grp", "det"), None),
        P("grp", "det", None),
        P("grp", "det", None),
        P("grp"),
    )
    out_specs = (P("grp", "det", None), P(("grp", "det"), None))
    body = functools.partial(shards, mesh.shape["det"])

    return jax.shard_map(body, mesh=mesh, in_specs=in_specs, out_specs=out_specs, check_vma=False)
```

```python
import functools
import math

import jax
import jax.numpy as jnp
from jax import lax
from jax.experimental import pallas as pl
from jax.experimental.pallas import tpu as pltpu
from jax.sharding import PartitionSpec as P


F32, BF16 = jnp.float32, jnp.bfloat16
ROWS = 8
UNITS = 8
LIMIT = pltpu.CompilerParams(vmem_limit_bytes=16 << 20)


def halves(value):
    high = value.astype(BF16)
    return high, (value - high.astype(F32)).astype(BF16)


def table_halves(table):
    high = lax.reduce_precision(table, exponent_bits=8, mantissa_bits=7)
    return high.astype(BF16), (table - high).astype(BF16)


def mm(a, b):
    return jnp.dot(a, b, preferred_element_type=F32)


def mm3(a_pair, b_pair):
    return mm(a_pair[0], b_pair[0]) + (mm(a_pair[1], b_pair[0]) + mm(a_pair[0], b_pair[1]))


def angles(count, first, second):
    return (first * second % count).astype(F32) * (2.0 * math.pi / count)


def section_table(side, unit_of_slot):
    unit = unit_of_slot[:, None, None]
    sample = lax.broadcasted_iota(jnp.int32, (1, 1, side), 2)
    part = lax.broadcasted_iota(jnp.int32, (1, 2, 1), 1)
    nyquist = (unit == 0) & (part == 1)
    angle = angles(side, jnp.where(nyquist, side // 2, unit), sample)
    table = jnp.where((part == 0) | nyquist, jnp.cos(angle), -jnp.sin(angle))
    return table.reshape(-1, side)


def inner_tables(side):
    first = lax.broadcasted_iota(jnp.int32, (side, side), 0)
    second = lax.broadcasted_iota(jnp.int32, (side, side), 1)
    angle = angles(side, first, second)
    cos, sin = jnp.cos(angle), jnp.sin(angle)
    forward = jnp.concatenate([jnp.concatenate([cos, -sin], 1), jnp.concatenate([sin, cos], 1)], 0)
    backward = jnp.concatenate([jnp.concatenate([cos, sin], 1), jnp.concatenate([-sin, cos], 1)], 0)
    return forward, backward


def twiddles(side):
    unit = lax.broadcasted_iota(jnp.int32, (side // 2 + 8, side), 0)
    sample = lax.broadcasted_iota(jnp.int32, (side // 2 + 8, side), 1)
    angle = angles(side * side, unit, sample)
    return jnp.cos(angle), jnp.sin(angle)


def section_kernel(side, x_ref, scale_ref, high_ref, low_ref, *refs):
    out_refs, (rows, turned) = refs[:-2], refs[-2:]
    scale = scale_ref[...]
    for n in range(side):
        rows[n * ROWS : (n + 1) * ROWS, :] = x_ref[:, n * side : (n + 1) * side] * scale
    table = (high_ref[...], low_ref[...])
    for d in range(0, ROWS, 2):
        pair = jnp.concatenate([rows[pl.ds(d, side, stride=ROWS), :], rows[pl.ds(d + 1, side, stride=ROWS), :]], axis=1)
        result = mm3(table, halves(pair))
        turned[pl.ds(d, len(result), stride=ROWS), :] = result[:, :side]
        turned[pl.ds(d + 1, len(result), stride=ROWS), :] = result[:, side:]
    lines = [(out_ref, row) for out_ref in out_refs for row in range(out_ref.shape[0])]
    for k, (out_ref, row) in enumerate(lines):
        out_ref[row] = turned[k * ROWS : (k + 1) * ROWS, :]


def sections(signal, scale, table, shares):
    dets, samples = signal.shape
    side = table.shape[1]
    high, low = table_halves(table)
    whole = pl.BlockSpec(table.shape, lambda i: (0, 0))
    return pl.pallas_call(
        functools.partial(section_kernel, side),
        grid=(dets // ROWS,),
        in_specs=[pl.BlockSpec((ROWS, samples), lambda i: (i, 0)), pl.BlockSpec((ROWS, side), lambda i: (i, 0)), whole, whole],
        out_specs=[pl.BlockSpec((share, ROWS, side), lambda i: (0, i, 0)) for share in shares],
        out_shape=[jax.ShapeDtypeStruct((share, dets, side), F32) for share in shares],
        scratch_shapes=[pltpu.VMEM((side * ROWS, side), F32), pltpu.VMEM((sum(shares) * ROWS, side), F32)],
        compiler_params=LIMIT,
        name="sections",
    )(signal, scale, high, low)


def cost(passes, rows, depth, columns, *arrays):
    moved = sum(array.size * array.dtype.itemsize for array in arrays)
    return pl.CostEstimate(flops=2 * passes * rows * depth * columns, bytes_accessed=moved, transcendentals=0)


def coeff_kernel(z_ref, high_ref, low_ref, out_ref, z_high, z_low):
    blocks, rows, dets, side = z_ref.shape
    for b in range(blocks):
        for k in range(rows):
            high, low = halves(z_ref[b, k])
            z_high[b * dets : (b + 1) * dets, k * side : (k + 1) * side] = high
            z_low[b * dets : (b + 1) * dets, k * side : (k + 1) * side] = low
    total = mm3((high_ref[...], low_ref[...]), (z_high[...], z_low[...]))
    for k in range(rows):
        out_ref[k] = total[:, k * side : (k + 1) * side]


def coefficients(slab, weights):
    blocks, rows, dets, side = slab.shape
    rank = weights[0].shape[0]
    out = jax.ShapeDtypeStruct((rows, rank, side), F32)
    step = math.gcd(2, rows)
    whole = pl.BlockSpec((rank, blocks * dets), lambda i: (0, 0))
    return pl.pallas_call(
        coeff_kernel,
        grid=(rows // step,),
        in_specs=[pl.BlockSpec((blocks, step, dets, side), lambda i: (0, i, 0, 0)), whole, whole],
        out_specs=pl.BlockSpec((step, rank, side), lambda i: (i, 0, 0)),
        out_shape=out,
        scratch_shapes=[pltpu.VMEM((blocks * dets, step * side), BF16)] * 2,
        compiler_params=LIMIT,
        cost_estimate=cost(3, rank, blocks * dets, rows * side, slab, out),
        name="coefficients",
    )(slab, *weights)


def correct_kernel(terms, z_ref, *refs):
    c_refs, (high_ref, low_ref, out_ref) = refs[:terms], refs[terms:]
    blocks, rows, dets, side = z_ref.shape
    coeff = halves(jnp.concatenate([sum(c_ref[k] for c_ref in c_refs) for k in range(rows)], axis=1))
    share = mm3((high_ref[...], low_ref[...]), coeff)
    for b in range(blocks):
        for k in range(rows):
            out_ref[b, k] = z_ref[b, k] - share[b * dets : (b + 1) * dets, k * side : (k + 1) * side]


def corrected(slab, coeffs, pattern):
    blocks, rows, dets, side = slab.shape
    rank = pattern[0].shape[1]
    step = math.gcd(2, rows)
    whole = pl.BlockSpec((blocks * dets, rank), lambda i: (0, 0))
    block = pl.BlockSpec((blocks, step, dets, side), lambda i: (0, i, 0, 0))
    return pl.pallas_call(
        functools.partial(correct_kernel, len(coeffs)),
        grid=(rows // step,),
        in_specs=[block] + [pl.BlockSpec((step, rank, side), lambda i: (i, 0, 0)) for _ in coeffs] + [whole, whole],
        out_specs=block,
        out_shape=jax.ShapeDtypeStruct(slab.shape, F32),
        compiler_params=LIMIT,
        cost_estimate=cost(3, rank, blocks * dets, rows * side, slab, slab, *coeffs),
        name="corrected",
    )(pltpu.with_memory_space_constraint(slab, pltpu.HBM), *coeffs, *pattern)


def section_lines(group, section_ref, d, rows):
    pair = [group[pl.ds(d + e, rows, stride=ROWS), :] for e in (0, 1)]
    high, low = halves(jnp.concatenate(pair, axis=1))
    return mm(section_ref[...], jnp.concatenate([high, low, high], axis=0))


def synth_kernel(base, count, steps, z_ref, w_ref, extra_ref, turn_ref, tables_ref, section_ref, rows_ref, hits_ref, *refs):
    *ends, t_high, t_low, result, held, tile_high, tile_low, total_ref, one = refs
    ending = len(ends) == 4
    _, dets, side = z_ref.shape
    step = pl.program_id(0)

    @pl.when(step < steps)
    def _():
        first = base + step * count
        has_zero = base == 0

        def turn(unit):
            pair = turn_ref[pl.ds(unit, 1), :]
            return pair[:, :side], pair[:, side:]

        half_cos, half_sin = turn(side // 2)
        turns = [turn(first + i) for i in range(count)]
        table = lambda i: tables_ref[i * 2 * side : (i + 1) * 2 * side, :]

        def put(slot, real, imag):
            for part, value in ((0, real), (1, imag)):
                high, low = halves(value)
                t_high[slot * dets : (slot + 1) * dets, part * side : (part + 1) * side] = high
                t_low[slot * dets : (slot + 1) * dets, part * side : (part + 1) * side] = low

        def transform(high, low):
            middle = result.shape[0] // 2 // 16 * 16
            for at in (slice(0, middle), slice(middle, result.shape[0])):
                result[at] = mm3((t_high[at], t_low[at]), (table(high), table(low)))

        for i in range(count):
            real, imag = z_ref[2 * i], z_ref[2 * i + 1]
            if has_zero and i == 0:
                put(count, imag * half_cos, -imag * half_sin)
                imag = jnp.where(first == 0, 0.0, imag)
            cos, sin = turns[i]
            put(i, real * cos + imag * sin, imag * cos - real * sin)
        transform(0, 1)
        for i in range(count + has_zero):
            weight = extra_ref[...] if i == count else w_ref[i]
            at = slice(i * dets, (i + 1) * dets)
            put(i, result[at, :side] * weight, result[at, side:] * weight)
        transform(2, 3)
        for i in range(count):
            at = slice(i * dets, (i + 1) * dets)
            real, imag = result[at, :side], result[at, side:]
            cos, sin = turns[i]
            turned = imag * cos + real * sin
            if has_zero and i == 0:
                at = slice(count * dets, (count + 1) * dets)
                nyquist = result[at, :side] * half_cos - result[at, side:] * half_sin
                turned = jnp.where(first == 0, nyquist, turned)
            for part, value in ((0, real * cos - imag * sin), (1, turned)):
                row = pl.multiple_of((2 * (step * count + i) + part) * ROWS, ROWS)
                for group in range(dets // ROWS):
                    held[group, pl.ds(row, ROWS), :] = value[group * ROWS : (group + 1) * ROWS]

    @pl.when(step >= steps)
    def _():
        rows = 2 * count * steps
        tiles = tile_high.shape[0] // ROWS
        group = held.at[step - steps]
        lines_ref = one if ending else ends[0]
        for d in range(0, ROWS, 2):
            lines = section_lines(group, section_ref, d, rows)
            for e in (0, 1):
                at = (d + e) * side
                lines_ref[at : at + side, :] = lines[:, e * side : (e + 1) * side]
                for half in (0, 1):
                    high, low = halves(lines_ref[pl.ds(at + half, side // 2, stride=2), :])
                    into = slice((d + e) * tiles, (d + e + 1) * tiles)
                    tile_high[into, half * side : (half + 1) * side] = high
                    tile_low[into, half * side : (half + 1) * side] = low
        if ending:
            ends[2][0] = group[...]
        sums_ref = total_ref if ending else ends[1]
        ladder = lax.broadcasted_iota(jnp.int32, (sums_ref.shape[0], ROWS * tiles), 0)
        chosen = jnp.where(rows_ref[0] == ladder, hits_ref[0], 0.0).astype(BF16)
        total = mm(chosen, tile_high[...]) + mm(chosen, tile_low[...])
        before = ends[0][...] if ending else 0.0
        sums_ref[...] = total + jnp.where(step == steps, before, sums_ref[...])
        if ending:
            _, tail_ref, _, parcel_ref = ends

            @pl.when(step == pl.num_programs(0) - 1)
            def _():
                own = sums_ref.shape[0] // parcel_ref.shape[0]
                for owner in range(parcel_ref.shape[0]):
                    parcel_ref[owner, :own] = sums_ref[owner * own : (owner + 1) * own, :]
                    parcel_ref[owner, own:] = tail_ref[owner]


def stacked(section):
    high, low = table_halves(section)
    return jnp.concatenate([high, high, low], axis=1)


def synth(base, slab, weight, extra, turns, tables, section, rows, hits, blocks, ending=()):
    lines, dets, side = slab.shape
    tiles = rows.size // dets
    count = math.gcd(lines // 2, UNITS)
    steps, groups = lines // (2 * count), dets // ROWS
    room = (count + (base == 0)) * dets
    whole = lambda a: pl.BlockSpec(a.shape, lambda i: (0,) * a.ndim)
    later = lambda i: jnp.maximum(i - steps, 0)
    line = pl.BlockSpec((1, 1, ROWS * tiles), lambda i: (later(i), 0, 0))
    slab, weight = [pltpu.with_memory_space_constraint(a, pltpu.HBM) for a in (slab, weight)]
    operands = [slab, weight, extra, turns, tables, section, rows.reshape(groups, 1, -1), hits.reshape(groups, 1, -1), *ending]
    in_specs = [
        pl.BlockSpec((2 * count, dets, side), lambda i: (jnp.minimum(i, steps - 1), 0, 0)),
        pl.BlockSpec((count, dets, side), lambda i: (base // count + jnp.minimum(i, steps - 1), 0, 0)),
        *[whole(a) for a in operands[2:6]],
        line,
        line,
        *[whole(a) for a in ending],
    ]
    if ending:
        _, tail = ending
        parcel = (tail.shape[0], blocks // tail.shape[0] + tail.shape[1], tail.shape[2])
        out = [jax.ShapeDtypeStruct((groups, lines * ROWS, side), F32), jax.ShapeDtypeStruct(parcel, F32)]
        out_specs = [pl.BlockSpec((1, lines * ROWS, side), lambda i: (later(i), 0, 0)), whole(out[1])]
    else:
        out = [jax.ShapeDtypeStruct((dets * side, side), F32), jax.ShapeDtypeStruct((blocks, 2 * side), F32)]
        out_specs = [pl.BlockSpec((ROWS * side, side), lambda i: (later(i), 0)), whole(out[1])]
    return pl.pallas_call(
        functools.partial(synth_kernel, base, count, steps),
        grid=(steps + groups,),
        in_specs=in_specs,
        out_specs=out_specs,
        out_shape=out,
        scratch_shapes=[
            *[pltpu.VMEM((room, 2 * side), BF16)] * 2,
            pltpu.VMEM((room, 2 * side), F32),
            pltpu.VMEM((groups, lines * ROWS, side), F32),
            *[pltpu.VMEM((ROWS * tiles, 2 * side), BF16)] * 2,
            pltpu.VMEM((blocks, 2 * side), F32),
            pltpu.VMEM((ROWS * side, side), F32),
        ],
        compiler_params=LIMIT,
        cost_estimate=cost(8, lines // 2 * dets, 2 * side, 2 * side, slab, slab, out[0]),
        name="synth",
    )(*operands)


def emit_kernel(before_ref, held_ref, section_ref, out_ref, lined):
    side = before_ref.shape[1]
    rows = held_ref.shape[1] // ROWS
    for d in range(0, ROWS, 2):
        lines = section_lines(held_ref.at[0], section_ref, d, rows)
        for e in (0, 1):
            at = (d + e) * side
            line = lines[:, e * side : (e + 1) * side] + before_ref[at : at + side, :]
            lined[pl.ds(d + e, side, stride=ROWS), :] = line
    for n in range(side):
        out_ref[:, n * side : (n + 1) * side] = lined[n * ROWS : (n + 1) * ROWS, :]


def emit(before, held, section):
    groups, lines, side = held.shape
    out = jax.ShapeDtypeStruct((groups * ROWS, side * side), F32)
    return pl.pallas_call(
        emit_kernel,
        grid=(groups,),
        in_specs=[
            pl.BlockSpec((ROWS * side, side), lambda i: (i, 0)),
            pl.BlockSpec((1, lines, side), lambda i: (i, 0, 0)),
            pl.BlockSpec(section.shape, lambda i: (0, 0)),
        ],
        out_specs=pl.BlockSpec((ROWS, side * side), lambda i: (i, 0)),
        out_shape=out,
        scratch_shapes=[pltpu.VMEM((ROWS * side, side), F32)],
        compiler_params=LIMIT,
        cost_estimate=cost(1, side, lines // ROWS, ROWS * groups * side, before, held, out),
        name="emit",
    )(pltpu.with_memory_space_constraint(before, pltpu.HBM), held, section)


def shards(size, timestream, gains, mode_pattern, mode_weights, noise_weight, block_ids, hits, sky_rows):
    _, dets, samples = timestream.shape
    side = math.isqrt(samples)
    units = side // 2
    blocks = sky_rows.shape[0]
    half = size // 2
    quarter = size // 4
    groups = [list(range(half)), [*range(half + quarter, size), *range(half, half + quarter)]]
    opposite = [*zip(groups[0], groups[1]), *zip(groups[1], groups[0])]
    mine = lax.axis_index("det") // half

    scale = jnp.broadcast_to(1.0 / gains.reshape(dets, 1), (dets, side))
    table = section_table(side, lax.iota(jnp.int32, units))
    share = side // 2
    parts = [table[:share], table[share:]]
    stacks = [stacked(part.T / samples) for part in parts]
    z = []
    for part in parts:
        z += sections(timestream.reshape(dets, samples), scale, part, [share])

    def of_half(modes):
        modes = modes.reshape(4, quarter * dets, -1)
        parts = [lax.dynamic_index_in_dim(modes, at, 0, keepdims=False) for at in (3 * mine, 1 + mine)]
        return jnp.concatenate(parts, axis=0)

    weights = table_halves(of_half(mode_weights).T)
    pattern = table_halves(of_half(mode_pattern))
    w = jnp.transpose(noise_weight.reshape(dets, side, side), (2, 0, 1))
    mirror = w[:units:-1, :, ::-1]
    weight = jnp.concatenate([w[:1], w[1:units] + mirror], axis=0)
    extra = w[units]
    forward, backward = inner_tables(side)
    tables = jnp.concatenate([*table_halves(forward), *table_halves(backward)], axis=0)
    turns = jnp.concatenate(twiddles(side), axis=1)

    ids_flat = block_ids.reshape(-1)
    ladder = lax.broadcasted_iota(jnp.int32, (blocks, ids_flat.shape[0]), 0)
    rows = jnp.sum(jnp.where(ids_flat[None, :] == ladder, sky_rows[:, None], 0), axis=0)
    hit = hits.reshape(-1).astype(F32)
    counts = jnp.sum(jnp.where(rows[None, :] == ladder, hit[None, :], 0.0), axis=1)

    own = blocks // size
    tail = jnp.pad(counts.reshape(size, 1, own), ((0, 0), (0, ROWS - 1), (0, 2 * side - own)))

    last = [None]

    def exchange(value):
        if last[0] is not None:
            value, _ = lax.optimization_barrier((value, last[0]))
        last[0] = lax.all_to_all(value, "det", split_axis=0, concat_axis=0, axis_index_groups=groups, tiled=True)
        return last[0]

    slabs, coeffs, others = [], [], []
    for c in (0, 1):
        slabs.append(exchange(z[c]).reshape(half, share // half, dets, side))
        coeffs.append(coefficients(slabs[c], weights))
        others.append(lax.ppermute(coeffs[c], "det", opposite))
    for c in (0, 1):
        slab = corrected(slabs[c], [coeffs[c], others[c]], pattern)
        back = exchange(slab.reshape(share, dets, side))
        operands = [c * units // 2, back, weight, extra, turns, tables, stacks[c], rows, hit, blocks]
        if c == 0:
            lines, sums = synth(*operands)
        else:
            held, parcel = synth(*operands, ending=(sums, tail))

    parcel = lax.all_to_all(parcel, "det", split_axis=0, concat_axis=0, tiled=True)
    filtered = emit(lines, held, stacks[1])
    parcel = jnp.sum(parcel, axis=0)
    sky_map = parcel[:own] / jnp.sqrt(1.0 + parcel[own, :own])[:, None]
    return filtered.reshape(timestream.shape), sky_map


def solution(mesh):
    in_specs = (
        P("grp", "det", None),
        P("grp", "det"),
        P("grp", None),
        P("grp", None),
        P(("grp", "det"), None),
        P("grp", "det", None),
        P("grp", "det", None),
        P("grp"),
    )
    out_specs = (P("grp", "det", None), P(("grp", "det"), None))
    body = functools.partial(shards, mesh.shape["det"])

    return jax.shard_map(body, mesh=mesh, in_specs=in_specs, out_specs=out_specs, check_vma=False)
```

```python
import functools
import math

import jax
import jax.numpy as jnp
from jax import lax
from jax.experimental import pallas as pl
from jax.experimental.pallas import tpu as pltpu
from jax.sharding import PartitionSpec as P


F32, BF16 = jnp.float32, jnp.bfloat16
ROWS = 8
UNITS = 8
LIMIT = pltpu.CompilerParams(vmem_limit_bytes=16 << 20)


def halves(value):
    high = value.astype(BF16)
    return high, (value - high.astype(F32)).astype(BF16)


def table_halves(table):
    high = lax.reduce_precision(table, exponent_bits=8, mantissa_bits=7)
    return high.astype(BF16), (table - high).astype(BF16)


def mm(a, b):
    return jnp.dot(a, b, preferred_element_type=F32)


def mm3(a_pair, b_pair):
    return mm(a_pair[0], b_pair[0]) + (mm(a_pair[1], b_pair[0]) + mm(a_pair[0], b_pair[1]))


def angles(count, first, second):
    return (first * second % count).astype(F32) * (2.0 * math.pi / count)


def section_table(side, unit_of_slot):
    unit = unit_of_slot[:, None, None]
    sample = lax.broadcasted_iota(jnp.int32, (1, 1, side), 2)
    part = lax.broadcasted_iota(jnp.int32, (1, 2, 1), 1)
    nyquist = (unit == 0) & (part == 1)
    angle = angles(side, jnp.where(nyquist, side // 2, unit), sample)
    table = jnp.where((part == 0) | nyquist, jnp.cos(angle), -jnp.sin(angle))
    return table.reshape(-1, side)


def inner_tables(side):
    first = lax.broadcasted_iota(jnp.int32, (side, side), 0)
    second = lax.broadcasted_iota(jnp.int32, (side, side), 1)
    angle = angles(side, first, second)
    cos, sin = jnp.cos(angle), jnp.sin(angle)
    forward = jnp.concatenate([jnp.concatenate([cos, -sin], 1), jnp.concatenate([sin, cos], 1)], 0)
    backward = jnp.concatenate([jnp.concatenate([cos, sin], 1), jnp.concatenate([-sin, cos], 1)], 0)
    return forward, backward


def twiddles(side):
    unit = lax.broadcasted_iota(jnp.int32, (side // 2 + 8, side), 0)
    sample = lax.broadcasted_iota(jnp.int32, (side // 2 + 8, side), 1)
    angle = angles(side * side, unit, sample)
    return jnp.cos(angle), jnp.sin(angle)


def section_kernel(side, x_ref, scale_ref, high_ref, low_ref, *refs):
    out_refs, (rows, turned) = refs[:-2], refs[-2:]
    scale = scale_ref[...]
    for n in range(side):
        rows[n * ROWS : (n + 1) * ROWS, :] = x_ref[:, n * side : (n + 1) * side] * scale
    table = (high_ref[...], low_ref[...])
    for d in range(0, ROWS, 2):
        pair = jnp.concatenate([rows[pl.ds(d, side, stride=ROWS), :], rows[pl.ds(d + 1, side, stride=ROWS), :]], axis=1)
        result = mm3(table, halves(pair))
        turned[pl.ds(d, len(result), stride=ROWS), :] = result[:, :side]
        turned[pl.ds(d + 1, len(result), stride=ROWS), :] = result[:, side:]
    lines = [(out_ref, row) for out_ref in out_refs for row in range(out_ref.shape[0])]
    for k, (out_ref, row) in enumerate(lines):
        out_ref[row] = turned[k * ROWS : (k + 1) * ROWS, :]


def sections(signal, scale, table, shares):
    dets, samples = signal.shape
    side = table.shape[1]
    high, low = table_halves(table)
    whole = pl.BlockSpec(table.shape, lambda i: (0, 0))
    return pl.pallas_call(
        functools.partial(section_kernel, side),
        grid=(dets // ROWS,),
        in_specs=[pl.BlockSpec((ROWS, samples), lambda i: (i, 0)), pl.BlockSpec((ROWS, side), lambda i: (i, 0)), whole, whole],
        out_specs=[pl.BlockSpec((share, ROWS, side), lambda i: (0, i, 0)) for share in shares],
        out_shape=[jax.ShapeDtypeStruct((share, dets, side), F32) for share in shares],
        scratch_shapes=[pltpu.VMEM((side * ROWS, side), F32), pltpu.VMEM((sum(shares) * ROWS, side), F32)],
        compiler_params=LIMIT,
        name="sections",
    )(signal, scale, high, low)


def cost(passes, rows, depth, columns, *arrays):
    moved = sum(array.size * array.dtype.itemsize for array in arrays)
    return pl.CostEstimate(flops=2 * passes * rows * depth * columns, bytes_accessed=moved, transcendentals=0)


def block_reader(me_ref, z_refs):
    if len(z_refs) > 1:
        return lambda b, k: z_refs[b][k]
    return lambda b, k: z_refs[0][me_ref[0] ^ b, k]


def slab_specs(slab, step):
    if len(slab) > 1:
        return [pl.BlockSpec((step,) + piece.shape[1:], lambda i: (i, 0, 0)) for piece in slab]
    blocks, _, dets, side = slab[0].shape
    return [pl.BlockSpec((blocks, step, dets, side), lambda i: (0, i, 0, 0))]


def coeff_kernel(blocks, me_ref, *refs):
    *z_refs, high_ref, low_ref, out_ref, z_high, z_low = refs
    rows, dets, side = z_refs[0].shape[-3:]
    block = block_reader(me_ref, z_refs)
    for b in range(blocks):
        for k in range(rows):
            high, low = halves(block(b, k))
            z_high[b * dets : (b + 1) * dets, k * side : (k + 1) * side] = high
            z_low[b * dets : (b + 1) * dets, k * side : (k + 1) * side] = low
    total = mm3((high_ref[...], low_ref[...]), (z_high[...], z_low[...]))
    for k in range(rows):
        out_ref[k] = total[:, k * side : (k + 1) * side]


SCALAR = pl.BlockSpec(memory_space=pltpu.SMEM)


def coefficients(me, slab, weights):
    rows, dets, side = slab[0].shape[-3:]
    rank, depth = weights[0].shape
    out = jax.ShapeDtypeStruct((rows, rank, side), F32)
    step = math.gcd(2, rows)
    whole = pl.BlockSpec((rank, depth), lambda i: (0, 0))
    return pl.pallas_call(
        functools.partial(coeff_kernel, depth // dets),
        grid=(rows // step,),
        in_specs=[SCALAR] + slab_specs(slab, step) + [whole, whole],
        out_specs=pl.BlockSpec((step, rank, side), lambda i: (i, 0, 0)),
        out_shape=out,
        scratch_shapes=[pltpu.VMEM((depth, step * side), BF16)] * 2,
        compiler_params=LIMIT,
        cost_estimate=cost(3, rank, depth, rows * side, out, *slab),
        name="coefficients",
    )(me, *slab, *weights)


def correct_kernel(pieces, terms, me_ref, *refs):
    z_refs, c_refs = refs[:pieces], refs[pieces : pieces + terms]
    high_ref, low_ref, *out_refs = refs[pieces + terms :]
    rows, dets, side = z_refs[0].shape[-3:]
    block = block_reader(me_ref, z_refs)
    coeff = halves(jnp.concatenate([sum(c_ref[k] for c_ref in c_refs) for k in range(rows)], axis=1))
    share = mm3((high_ref[...], low_ref[...]), coeff)
    for b in range(share.shape[0] // dets):
        for k in range(rows):
            value = block(b, k) - share[b * dets : (b + 1) * dets, k * side : (k + 1) * side]
            if len(out_refs) > 1:
                out_refs[b][k] = value
            else:
                out_refs[0][me_ref[0] ^ b, k] = value


def corrected(me, slab, coeffs, pattern, apart):
    rows, dets, side = slab[0].shape[-3:]
    depth, rank = pattern[0].shape
    blocks = depth // dets
    step = math.gcd(2, rows)
    whole = pl.BlockSpec((depth, rank), lambda i: (0, 0))
    if apart:
        out = [jax.ShapeDtypeStruct((rows, dets, side), F32)] * blocks
    else:
        out = [jax.ShapeDtypeStruct((blocks, rows, dets, side), F32)]
        slab = slab[:]
    return pl.pallas_call(
        functools.partial(correct_kernel, len(slab), len(coeffs)),
        grid=(rows // step,),
        in_specs=[SCALAR]
        + slab_specs(slab, step)
        + [pl.BlockSpec((step, rank, side), lambda i: (i, 0, 0)) for _ in coeffs]
        + [whole, whole],
        out_specs=slab_specs(out, step),
        out_shape=out,
        compiler_params=LIMIT,
        cost_estimate=cost(3, rank, depth, rows * side, *slab, *out, *coeffs),
        name="corrected",
    )(me, *[pltpu.with_memory_space_constraint(a, pltpu.HBM) for a in slab], *coeffs, *pattern)


def section_lines(group, section_ref, d, rows):
    pair = [group[pl.ds(d + e, rows, stride=ROWS), :] for e in (0, 1)]
    high, low = halves(jnp.concatenate(pair, axis=1))
    return mm(section_ref[...], jnp.concatenate([high, low, high], axis=0))


def synth_kernel(base, count, steps, pieces, me_ref, *refs):
    z_refs, refs = refs[:pieces], refs[pieces:]
    w_ref, extra_ref, turn_ref, tables_ref, section_ref, rows_ref, hits_ref, *refs = refs
    *ends, t_high, t_low, result, held, tile_high, tile_low, total_ref, one = refs
    ending = len(ends) == 4
    dets, side = z_refs[0].shape[-2:]
    step = pl.program_id(0)
    has_zero = base == 0

    def turn(unit):
        pair = turn_ref[pl.ds(unit, 1), :]
        return pair[:, :side], pair[:, side:]

    def put(slot, real, imag):
        for part, value in ((0, real), (1, imag)):
            high, low = halves(value)
            t_high[slot * dets : (slot + 1) * dets, part * side : (part + 1) * side] = high
            t_low[slot * dets : (slot + 1) * dets, part * side : (part + 1) * side] = low

    def transform(high, low):
        table = lambda i: tables_ref[i * 2 * side : (i + 1) * 2 * side, :]
        middle = result.shape[0] // 2 // 16 * 16
        for at in (slice(0, middle), slice(middle, result.shape[0])):
            result[at] = mm3((t_high[at], t_low[at]), (table(high), table(low)))

    def weigh(units, read):
        half_cos, half_sin = turn(side // 2)
        turns = [turn(base + unit) for unit in units]
        for i in range(count):
            real, imag = read(i)
            if has_zero and i == 0:
                put(count, imag * half_cos, -imag * half_sin)
                imag = jnp.where(units[0] == 0, 0.0, imag)
            cos, sin = turns[i]
            put(i, real * cos + imag * sin, imag * cos - real * sin)
        transform(0, 1)
        for i in range(count + has_zero):
            weight = extra_ref[...] if i == count else w_ref[i if pieces == 1 else units[i]]
            at = slice(i * dets, (i + 1) * dets)
            put(i, result[at, :side] * weight, result[at, side:] * weight)
        transform(2, 3)
        for i in range(count):
            at = slice(i * dets, (i + 1) * dets)
            real, imag = result[at, :side], result[at, side:]
            cos, sin = turns[i]
            turned = imag * cos + real * sin
            if has_zero and i == 0:
                at = slice(count * dets, (count + 1) * dets)
                nyquist = result[at, :side] * half_cos - result[at, side:] * half_sin
                turned = jnp.where(units[0] == 0, nyquist, turned)
            for part, value in ((0, real * cos - imag * sin), (1, turned)):
                row = pl.multiple_of((2 * units[i] + part) * ROWS, ROWS)
                for group in range(dets // ROWS):
                    held[group, pl.ds(row, ROWS), :] = value[group * ROWS : (group + 1) * ROWS]

    if pieces == 1:

        @pl.when(step < steps)
        def _():
            z_ref = z_refs[0]
            weigh([step * count + i for i in range(count)], lambda i: (z_ref[2 * i], z_ref[2 * i + 1]))

    else:
        each = z_refs[0].shape[0] // 2
        for at in range(steps):

            @pl.when(step == at)
            def _(at=at):
                slots = [divmod(at * count + i, each) for i in range(count)]
                weigh(
                    [(me_ref[0] ^ piece) * each + unit for piece, unit in slots],
                    lambda i: (z_refs[slots[i][0]][2 * slots[i][1]], z_refs[slots[i][0]][2 * slots[i][1] + 1]),
                )

    @pl.when(step >= steps)
    def _():
        rows = 2 * count * steps
        tiles = tile_high.shape[0] // ROWS
        group = held.at[step - steps]
        lines_ref = one if ending else ends[0]
        for d in range(0, ROWS, 2):
            lines = section_lines(group, section_ref, d, rows)
            for e in (0, 1):
                at = (d + e) * side
                lines_ref[at : at + side, :] = lines[:, e * side : (e + 1) * side]
                for half in (0, 1):
                    high, low = halves(lines_ref[pl.ds(at + half, side // 2, stride=2), :])
                    into = slice((d + e) * tiles, (d + e + 1) * tiles)
                    tile_high[into, half * side : (half + 1) * side] = high
                    tile_low[into, half * side : (half + 1) * side] = low
        if ending:
            ends[2][0] = group[...]
        sums_ref = total_ref if ending else ends[1]
        ladder = lax.broadcasted_iota(jnp.int32, (sums_ref.shape[0], ROWS * tiles), 0)
        chosen = jnp.where(rows_ref[0] == ladder, hits_ref[0], 0.0).astype(BF16)
        total = mm(chosen, tile_high[...]) + mm(chosen, tile_low[...])
        before = ends[0][...] if ending else 0.0
        sums_ref[...] = total + jnp.where(step == steps, before, sums_ref[...])
        if ending:
            _, tail_ref, _, parcel_ref = ends

            @pl.when(step == pl.num_programs(0) - 1)
            def _():
                own = sums_ref.shape[0] // parcel_ref.shape[0]
                for owner in range(parcel_ref.shape[0]):
                    parcel_ref[owner, :own] = sums_ref[owner * own : (owner + 1) * own, :]
                    parcel_ref[owner, own:] = tail_ref[owner]


def stacked(section):
    high, low = table_halves(section)
    return jnp.concatenate([high, high, low], axis=1)


def synth(me, base, slab, weight, extra, turns, tables, section, rows, hits, blocks, ending=()):
    pieces = len(slab)
    lines, dets, side = pieces * slab[0].shape[0], *slab[0].shape[1:]
    tiles = rows.size // dets
    count = math.gcd(lines // 2, UNITS)
    steps, groups = lines // (2 * count), dets // ROWS
    room = (count + (base == 0)) * dets
    whole = lambda a: pl.BlockSpec(a.shape, lambda i: (0,) * a.ndim)
    later = lambda i: jnp.maximum(i - steps, 0)
    line = pl.BlockSpec((1, 1, ROWS * tiles), lambda i: (later(i), 0, 0))
    weight = pltpu.with_memory_space_constraint(weight, pltpu.HBM)
    others = [extra, turns, tables, section]
    if pieces == 1:
        slab = [pltpu.with_memory_space_constraint(slab[0], pltpu.HBM)]
        z_specs = [pl.BlockSpec((2 * count, dets, side), lambda i: (jnp.minimum(i, steps - 1), 0, 0))]
        w_spec = pl.BlockSpec((count, dets, side), lambda i: (base // count + jnp.minimum(i, steps - 1), 0, 0))
    else:
        z_specs = [whole(piece) for piece in slab]
        w_spec = pl.BlockSpec((lines // 2, dets, side), lambda i: (2 * base // lines, 0, 0))
    operands = [me, *slab, weight, *others, rows.reshape(groups, 1, -1), hits.reshape(groups, 1, -1), *ending]
    in_specs = [
        SCALAR,
        *z_specs,
        w_spec,
        *[whole(a) for a in others],
        line,
        line,
        *[whole(a) for a in ending],
    ]
    if ending:
        _, tail = ending
        parcel = (tail.shape[0], blocks // tail.shape[0] + tail.shape[1], tail.shape[2])
        out = [jax.ShapeDtypeStruct((groups, lines * ROWS, side), F32), jax.ShapeDtypeStruct(parcel, F32)]
        out_specs = [pl.BlockSpec((1, lines * ROWS, side), lambda i: (later(i), 0, 0)), whole(out[1])]
    else:
        out = [jax.ShapeDtypeStruct((dets * side, side), F32), jax.ShapeDtypeStruct((blocks, 2 * side), F32)]
        out_specs = [pl.BlockSpec((ROWS * side, side), lambda i: (later(i), 0)), whole(out[1])]
    return pl.pallas_call(
        functools.partial(synth_kernel, base, count, steps, pieces),
        grid=(steps + groups,),
        in_specs=in_specs,
        out_specs=out_specs,
        out_shape=out,
        scratch_shapes=[
            *[pltpu.VMEM((room, 2 * side), BF16)] * 2,
            pltpu.VMEM((room, 2 * side), F32),
            pltpu.VMEM((groups, lines * ROWS, side), F32),
            *[pltpu.VMEM((ROWS * tiles, 2 * side), BF16)] * 2,
            pltpu.VMEM((blocks, 2 * side), F32),
            pltpu.VMEM((ROWS * side, side), F32),
        ],
        compiler_params=LIMIT,
        cost_estimate=cost(8, lines // 2 * dets, 2 * side, 2 * side, *slab, *slab, out[0]),
        name="synth",
    )(*operands)


def emit_kernel(before_ref, held_ref, section_ref, out_ref, lined):
    side = before_ref.shape[1]
    rows = held_ref.shape[1] // ROWS
    for d in range(0, ROWS, 2):
        lines = section_lines(held_ref.at[0], section_ref, d, rows)
        for e in (0, 1):
            at = (d + e) * side
            line = lines[:, e * side : (e + 1) * side] + before_ref[at : at + side, :]
            lined[pl.ds(d + e, side, stride=ROWS), :] = line
    for n in range(side):
        out_ref[:, n * side : (n + 1) * side] = lined[n * ROWS : (n + 1) * ROWS, :]


def emit(before, held, section):
    groups, lines, side = held.shape
    out = jax.ShapeDtypeStruct((groups * ROWS, side * side), F32)
    return pl.pallas_call(
        emit_kernel,
        grid=(groups,),
        in_specs=[
            pl.BlockSpec((ROWS * side, side), lambda i: (i, 0)),
            pl.BlockSpec((1, lines, side), lambda i: (i, 0, 0)),
            pl.BlockSpec(section.shape, lambda i: (0, 0)),
        ],
        out_specs=pl.BlockSpec((ROWS, side * side), lambda i: (i, 0)),
        out_shape=out,
        scratch_shapes=[pltpu.VMEM((ROWS * side, side), F32)],
        compiler_params=LIMIT,
        cost_estimate=cost(1, side, lines // ROWS, ROWS * groups * side, before, held, out),
        name="emit",
    )(pltpu.with_memory_space_constraint(before, pltpu.HBM), held, section)


def shards(size, timestream, gains, mode_pattern, mode_weights, noise_weight, block_ids, hits, sky_rows):
    _, dets, samples = timestream.shape
    side = math.isqrt(samples)
    units = side // 2
    blocks = sky_rows.shape[0]
    half = size // 2
    quarter = size // 4
    groups = [list(range(half)), [*range(half + quarter, size), *range(half, half + quarter)]]
    opposite = [*zip(groups[0], groups[1]), *zip(groups[1], groups[0])]
    mine = lax.axis_index("det") // half

    position = (lax.axis_index("det") % half + mine * quarter) % half
    me = position.reshape(1)

    scale = jnp.broadcast_to(1.0 / gains.reshape(dets, 1), (dets, side))
    share, each = side // 2, units // size
    number = lax.iota(jnp.int32, units // 2)
    table = section_table(side, lax.iota(jnp.int32, units))
    stacks = [stacked(part.T / samples) for part in (table[:share], table[share:])]
    parts = [section_table(side, (position ^ (number // each)) * each + number % each), table[share:]]
    z = []
    for part in parts:
        z += sections(timestream.reshape(dets, samples), scale, part, [share])

    def ordered(modes):
        modes = modes.reshape(size, dets, -1)
        at = [mine * half + (mine * quarter + (position ^ k)) % half for k in range(half)]
        return jnp.concatenate([lax.dynamic_index_in_dim(modes, i, 0, keepdims=False) for i in at], axis=0)

    weights = table_halves(ordered(mode_weights).T)
    pattern = table_halves(ordered(mode_pattern))
    w = jnp.transpose(noise_weight.reshape(dets, side, side), (2, 0, 1))
    mirror = w[:units:-1, :, ::-1]
    weight = jnp.concatenate([w[:1], w[1:units] + mirror], axis=0)
    extra = w[units]
    forward, backward = inner_tables(side)
    tables = jnp.concatenate([*table_halves(forward), *table_halves(backward)], axis=0)
    turns = jnp.concatenate(twiddles(side), axis=1)

    ids_flat = block_ids.reshape(-1)
    ladder = lax.broadcasted_iota(jnp.int32, (blocks, ids_flat.shape[0]), 0)
    rows = jnp.sum(jnp.where(ids_flat[None, :] == ladder, sky_rows[:, None], 0), axis=0)
    hit = hits.reshape(-1).astype(F32)
    counts = jnp.sum(jnp.where(rows[None, :] == ladder, hit[None, :], 0.0), axis=1)

    own = blocks // size
    tail = jnp.pad(counts.reshape(size, 1, own), ((0, 0), (0, ROWS - 1), (0, 2 * side - own)))

    last = [None]

    def exchange(value):
        if last[0] is not None:
            value, _ = lax.optimization_barrier((value, last[0]))
        last[0] = lax.all_to_all(value, "det", split_axis=0, concat_axis=0, axis_index_groups=groups, tiled=True)
        return last[0]

    reverse = lambda k: sum((half >> 1 >> bit) for bit in range(half.bit_length() - 1) if k >> bit & 1)

    def trade(pieces):
        found = list(pieces)
        for k in map(reverse, range(1, half)):
            pairs = [(group[p], group[p ^ k]) for group in groups for p in range(half)]
            found[k] = lax.ppermute(pieces[k], "det", pairs)
        return found

    slabs, coeffs, others = [], [], []
    for c in (0, 1):
        if c == 0:
            slab = trade([z[0][2 * each * k : 2 * each * (k + 1)] for k in range(half)])
            last[0] = slab[half - 1]
        else:
            slab = [exchange(z[1]).reshape(half, 2 * each, dets, side)]
        slabs.append(slab)
        coeffs.append(coefficients(me, slab, weights))
        others.append(lax.ppermute(coeffs[c], "det", opposite))
    for c in (0, 1):
        slab = corrected(me, slabs[c], [coeffs[c], others[c]], pattern, apart=c == 1)
        if c == 0:
            back = [exchange(slab[0].reshape(share, dets, side))]
        else:
            slab, _ = lax.optimization_barrier((slab, last[0]))
            back = trade(slab)
        operands = [me, c * units // 2, back, weight, extra, turns, tables, stacks[c], rows, hit, blocks]
        if c == 0:
            lines, sums = synth(*operands)
        else:
            held, parcel = synth(*operands, ending=(sums, tail))

    parcel = lax.all_to_all(parcel, "det", split_axis=0, concat_axis=0, tiled=True)
    filtered = emit(lines, held, stacks[1])
    parcel = jnp.sum(parcel, axis=0)
    sky_map = parcel[:own] / jnp.sqrt(1.0 + parcel[own, :own])[:, None]
    return filtered.reshape(timestream.shape), sky_map


def solution(mesh):
    in_specs = (
        P("grp", "det", None),
        P("grp", "det"),
        P("grp", None),
        P("grp", None),
        P(("grp", "det"), None),
        P("grp", "det", None),
        P("grp", "det", None),
        P("grp"),
    )
    out_specs = (P("grp", "det", None), P(("grp", "det"), None))
    body = functools.partial(shards, mesh.shape["det"])

    return jax.shard_map(body, mesh=mesh, in_specs=in_specs, out_specs=out_specs, check_vma=False)
```

```python
import functools
import math

import jax
import jax.numpy as jnp
from jax import lax
from jax.experimental import pallas as pl
from jax.experimental.pallas import tpu as pltpu
from jax.sharding import PartitionSpec as P


F32, BF16 = jnp.float32, jnp.bfloat16
ROWS = 8
UNITS = 8
ALL = pltpu.CompilerParams(vmem_limit_bytes=60 << 20)
LIMIT = pltpu.CompilerParams(vmem_limit_bytes=16 << 20)


def halves(value):
    high = value.astype(BF16)
    return high, (value - high.astype(F32)).astype(BF16)


def table_halves(table):
    high = lax.reduce_precision(table, exponent_bits=8, mantissa_bits=7)
    return high.astype(BF16), (table - high).astype(BF16)


def mm(a, b):
    return jnp.dot(a, b, preferred_element_type=F32)


def mm3(a_pair, b_pair):
    return mm(a_pair[0], b_pair[0]) + (mm(a_pair[1], b_pair[0]) + mm(a_pair[0], b_pair[1]))


def angles(count, first, second):
    return (first * second % count).astype(F32) * (2.0 * math.pi / count)


def section_table(side, unit_of_slot):
    unit = unit_of_slot[:, None, None]
    sample = lax.broadcasted_iota(jnp.int32, (1, 1, side), 2)
    part = lax.broadcasted_iota(jnp.int32, (1, 2, 1), 1)
    nyquist = (unit == 0) & (part == 1)
    angle = angles(side, jnp.where(nyquist, side // 2, unit), sample)
    table = jnp.where((part == 0) | nyquist, jnp.cos(angle), -jnp.sin(angle))
    return table.reshape(-1, side)


def inner_tables(side):
    first = lax.broadcasted_iota(jnp.int32, (side, side), 0)
    second = lax.broadcasted_iota(jnp.int32, (side, side), 1)
    angle = angles(side, first, second)
    cos, sin = jnp.cos(angle), jnp.sin(angle)
    forward = jnp.concatenate([jnp.concatenate([cos, -sin], 1), jnp.concatenate([sin, cos], 1)], 0)
    backward = jnp.concatenate([jnp.concatenate([cos, sin], 1), jnp.concatenate([-sin, cos], 1)], 0)
    return forward, backward


def twiddles(side):
    unit = lax.broadcasted_iota(jnp.int32, (side // 2 + 8, side), 0)
    sample = lax.broadcasted_iota(jnp.int32, (side // 2 + 8, side), 1)
    angle = angles(side * side, unit, sample)
    return jnp.cos(angle), jnp.sin(angle)


def section_kernel(side, x_ref, scale_ref, high_ref, low_ref, *refs):
    out_refs, (rows, turned) = refs[:-2], refs[-2:]
    scale = scale_ref[...]
    for n in range(side):
        rows[n * ROWS : (n + 1) * ROWS, :] = x_ref[:, n * side : (n + 1) * side] * scale
    table = (high_ref[...], low_ref[...])
    for d in range(0, ROWS, 2):
        pair = jnp.concatenate([rows[pl.ds(d, side, stride=ROWS), :], rows[pl.ds(d + 1, side, stride=ROWS), :]], axis=1)
        result = mm3(table, halves(pair))
        turned[pl.ds(d, len(result), stride=ROWS), :] = result[:, :side]
        turned[pl.ds(d + 1, len(result), stride=ROWS), :] = result[:, side:]
    lines = [(out_ref, row) for out_ref in out_refs for row in range(out_ref.shape[0])]
    for k, (out_ref, row) in enumerate(lines):
        out_ref[row] = turned[k * ROWS : (k + 1) * ROWS, :]


def sections(signal, scale, table, shares):
    dets, samples = signal.shape
    side = table.shape[1]
    high, low = table_halves(table)
    whole = pl.BlockSpec(table.shape, lambda i: (0, 0))
    return pl.pallas_call(
        functools.partial(section_kernel, side),
        grid=(dets // ROWS,),
        in_specs=[pl.BlockSpec((ROWS, samples), lambda i: (i, 0)), pl.BlockSpec((ROWS, side), lambda i: (i, 0)), whole, whole],
        out_specs=[pl.BlockSpec((share, ROWS, side), lambda i: (0, i, 0)) for share in shares],
        out_shape=[jax.ShapeDtypeStruct((share, dets, side), F32) for share in shares],
        scratch_shapes=[pltpu.VMEM((side * ROWS, side), F32), pltpu.VMEM((sum(shares) * ROWS, side), F32)],
        compiler_params=LIMIT,
        name="sections",
    )(signal, scale, high, low)


def cost(passes, rows, depth, columns, *arrays):
    moved = sum(array.size * array.dtype.itemsize for array in arrays)
    return pl.CostEstimate(flops=2 * passes * rows * depth * columns, bytes_accessed=moved, transcendentals=0)


def block_reader(me_ref, z_refs):
    if len(z_refs) > 1:
        return lambda b, k: z_refs[b][k]
    return lambda b, k: z_refs[0][me_ref[0] ^ b, k]


def slab_specs(slab, step):
    if len(slab) > 1:
        return [pl.BlockSpec((step,) + piece.shape[1:], lambda i: (i, 0, 0)) for piece in slab]
    blocks, _, dets, side = slab[0].shape
    return [pl.BlockSpec((blocks, step, dets, side), lambda i: (0, i, 0, 0))]


def coeff_kernel(blocks, me_ref, *refs):
    *z_refs, high_ref, low_ref, out_ref, z_high, z_low = refs
    rows, dets, side = z_refs[0].shape[-3:]
    block = block_reader(me_ref, z_refs)
    for b in range(blocks):
        for k in range(rows):
            high, low = halves(block(b, k))
            z_high[b * dets : (b + 1) * dets, k * side : (k + 1) * side] = high
            z_low[b * dets : (b + 1) * dets, k * side : (k + 1) * side] = low
    total = mm3((high_ref[...], low_ref[...]), (z_high[...], z_low[...]))
    for k in range(rows):
        out_ref[k] = total[:, k * side : (k + 1) * side]


SCALAR = pl.BlockSpec(memory_space=pltpu.SMEM)


def coefficients(me, slab, weights):
    rows, dets, side = slab[0].shape[-3:]
    rank, depth = weights[0].shape
    out = jax.ShapeDtypeStruct((rows, rank, side), F32)
    step = math.gcd(8, rows)
    whole = pl.BlockSpec((rank, depth), lambda i: (0, 0))
    return pl.pallas_call(
        functools.partial(coeff_kernel, depth // dets),
        grid=(rows // step,),
        in_specs=[SCALAR] + slab_specs(slab, step) + [whole, whole],
        out_specs=pl.BlockSpec((step, rank, side), lambda i: (i, 0, 0)),
        out_shape=out,
        scratch_shapes=[pltpu.VMEM((depth, step * side), BF16)] * 2,
        compiler_params=LIMIT,
        cost_estimate=cost(3, rank, depth, rows * side, out, *slab),
        name="coefficients",
    )(me, *slab, *weights)


def correct_kernel(pieces, terms, me_ref, *refs):
    z_refs, c_refs = refs[:pieces], refs[pieces : pieces + terms]
    high_ref, low_ref, *out_refs = refs[pieces + terms :]
    rows, dets, side = z_refs[0].shape[-3:]
    block = block_reader(me_ref, z_refs)
    coeff = halves(jnp.concatenate([sum(c_ref[k] for c_ref in c_refs) for k in range(rows)], axis=1))
    share = mm3((high_ref[...], low_ref[...]), coeff)
    for b in range(share.shape[0] // dets):
        for k in range(rows):
            value = block(b, k) - share[b * dets : (b + 1) * dets, k * side : (k + 1) * side]
            if len(out_refs) > 1:
                out_refs[b][k] = value
            else:
                out_refs[0][me_ref[0] ^ b, k] = value


def corrected(me, slab, coeffs, pattern, apart):
    rows, dets, side = slab[0].shape[-3:]
    depth, rank = pattern[0].shape
    blocks = depth // dets
    step = math.gcd(4, rows)
    whole = pl.BlockSpec((depth, rank), lambda i: (0, 0))
    if apart:
        out = [jax.ShapeDtypeStruct((rows, dets, side), F32)] * blocks
    else:
        out = [jax.ShapeDtypeStruct((blocks, rows, dets, side), F32)]
        slab = slab[:]
    return pl.pallas_call(
        functools.partial(correct_kernel, len(slab), len(coeffs)),
        grid=(rows // step,),
        in_specs=[SCALAR]
        + slab_specs(slab, step)
        + [pl.BlockSpec((step, rank, side), lambda i: (i, 0, 0)) for _ in coeffs]
        + [whole, whole],
        out_specs=slab_specs(out, step),
        out_shape=out,
        compiler_params=ALL if apart else LIMIT,
        cost_estimate=cost(3, rank, depth, rows * side, *slab, *out, *coeffs),
        name="corrected",
    )(me, *[pltpu.with_memory_space_constraint(a, pltpu.HBM) for a in slab], *coeffs, *pattern)


def section_lines(group, section_ref, d, rows):
    pair = [group[pl.ds(d + e, rows, stride=ROWS), :] for e in (0, 1)]
    high, low = halves(jnp.concatenate(pair, axis=1))
    return mm(section_ref[...], jnp.concatenate([high, low, high], axis=0))


def unit_filter(base, count, single, w_ref, extra_ref, turn_ref, tables_ref, t_high, t_low, result, held):
    dets, side = w_ref.shape[-2:]
    has_zero = base == 0

    def turn(unit):
        pair = turn_ref[pl.ds(unit, 1), :]
        return pair[:, :side], pair[:, side:]

    def put(slot, real, imag):
        for part, value in ((0, real), (1, imag)):
            high, low = halves(value)
            t_high[slot * dets : (slot + 1) * dets, part * side : (part + 1) * side] = high
            t_low[slot * dets : (slot + 1) * dets, part * side : (part + 1) * side] = low

    def transform(high, low):
        table = lambda i: tables_ref[i * 2 * side : (i + 1) * 2 * side, :]
        middle = result.shape[0] // 2 // 16 * 16
        for at in (slice(0, middle), slice(middle, result.shape[0])):
            result[at] = mm3((t_high[at], t_low[at]), (table(high), table(low)))

    def weigh(units, read):
        half_cos, half_sin = turn(side // 2)
        turns = [turn(base + unit) for unit in units]
        for i in range(count):
            real, imag = read(i)
            if has_zero and i == 0:
                put(count, imag * half_cos, -imag * half_sin)
                imag = jnp.where(units[0] == 0, 0.0, imag)
            cos, sin = turns[i]
            put(i, real * cos + imag * sin, imag * cos - real * sin)
        transform(0, 1)
        for i in range(count + has_zero):
            weight = extra_ref[...] if i == count else w_ref[i if single else units[i]]
            at = slice(i * dets, (i + 1) * dets)
            put(i, result[at, :side] * weight, result[at, side:] * weight)
        transform(2, 3)
        for i in range(count):
            at = slice(i * dets, (i + 1) * dets)
            real, imag = result[at, :side], result[at, side:]
            cos, sin = turns[i]
            turned = imag * cos + real * sin
            if has_zero and i == 0:
                at = slice(count * dets, (count + 1) * dets)
                nyquist = result[at, :side] * half_cos - result[at, side:] * half_sin
                turned = jnp.where(units[0] == 0, nyquist, turned)
            for part, value in ((0, real * cos - imag * sin), (1, turned)):
                row = pl.multiple_of((2 * units[i] + part) * ROWS, ROWS)
                for group in range(dets // ROWS):
                    held[group, pl.ds(row, ROWS), :] = value[group * ROWS : (group + 1) * ROWS]

    return weigh


def weigh_pieces(weigh, me_ref, z_refs, first, count, steps):
    step = pl.program_id(0)
    each = z_refs[0].shape[0] // 2
    for at in range(steps):

        @pl.when(step == at)
        def _(at=at):
            slots = [divmod(at * count + i, each) for i in range(count)]
            weigh(
                [(me_ref[0] ^ (first + piece)) * each + unit for piece, unit in slots],
                lambda i: (z_refs[slots[i][0]][2 * slots[i][1]], z_refs[slots[i][0]][2 * slots[i][1] + 1]),
            )


def early_kernel(base, count, steps, pieces, me_ref, *refs):
    z_refs, (w_ref, turn_ref, tables_ref, out_ref, t_high, t_low, result) = refs[:pieces], refs[pieces:]
    weigh = unit_filter(base, count, False, w_ref, None, turn_ref, tables_ref, t_high, t_low, result, out_ref)
    weigh_pieces(weigh, me_ref, z_refs, 0, count, steps)


def early(me, base, pieces, weight, turns, tables, count, lines):
    _, dets, side = pieces[0].shape
    steps = len(pieces) * pieces[0].shape[0] // (2 * count)
    out = jax.ShapeDtypeStruct((dets // ROWS, lines * ROWS, side), F32)
    whole = lambda a: pl.BlockSpec(a.shape, lambda i: (0,) * a.ndim)
    return pl.pallas_call(
        functools.partial(early_kernel, base, count, steps, len(pieces)),
        grid=(steps,),
        in_specs=[SCALAR]
        + [whole(piece) for piece in pieces]
        + [pl.BlockSpec((lines // 2, dets, side), lambda i: (2 * base // lines, 0, 0)), whole(turns), whole(tables)],
        out_specs=whole(out),
        out_shape=out,
        scratch_shapes=[pltpu.VMEM((count * dets, 2 * side), BF16)] * 2 + [pltpu.VMEM((count * dets, 2 * side), F32)],
        compiler_params=LIMIT,
        cost_estimate=cost(6, steps * count * dets, 2 * side, 2 * side, out, *pieces),
        name="early",
    )(me, *pieces, weight, turns, tables)


def synth_kernel(base, count, steps, first, pieces, me_ref, *refs):
    z_refs, refs = refs[:pieces], refs[pieces:]
    w_ref, extra_ref, turn_ref, tables_ref, section_ref, rows_ref, hits_ref, *refs = refs
    *ends, t_high, t_low, result, held, tile_high, tile_low, total_ref, one = refs
    if first:
        before_ref, *ends = ends
    ending = len(ends) == 4
    _, side = z_refs[0].shape[-2:]
    step = pl.program_id(0)
    weigh = unit_filter(
        base, count, pieces == 1 and not first, w_ref, extra_ref, turn_ref, tables_ref, t_high, t_low, result, held
    )
    if first:

        @pl.when(step == 0)
        def _():
            held[...] = before_ref[...]

    if pieces == 1 and not first:

        @pl.when(step < steps)
        def _():
            z_ref = z_refs[0]
            weigh([step * count + i for i in range(count)], lambda i: (z_ref[2 * i], z_ref[2 * i + 1]))

    else:
        weigh_pieces(weigh, me_ref, z_refs, first, count, steps)

    @pl.when(step >= steps)
    def _():
        rows = held.shape[1] // ROWS
        tiles = tile_high.shape[0] // ROWS
        group = held.at[step - steps]
        lines_ref = one if ending else ends[0]
        for d in range(0, ROWS, 2):
            lines = section_lines(group, section_ref, d, rows)
            for e in (0, 1):
                at = (d + e) * side
                lines_ref[at : at + side, :] = lines[:, e * side : (e + 1) * side]
                for half in (0, 1):
                    high, low = halves(lines_ref[pl.ds(at + half, side // 2, stride=2), :])
                    into = slice((d + e) * tiles, (d + e + 1) * tiles)
                    tile_high[into, half * side : (half + 1) * side] = high
                    tile_low[into, half * side : (half + 1) * side] = low
        if ending:
            ends[2][0] = group[...]
        sums_ref = total_ref if ending else ends[1]
        ladder = lax.broadcasted_iota(jnp.int32, (sums_ref.shape[0], ROWS * tiles), 0)
        chosen = jnp.where(rows_ref[0] == ladder, hits_ref[0], 0.0).astype(BF16)
        total = mm(chosen, tile_high[...]) + mm(chosen, tile_low[...])
        before = ends[0][...] if ending else 0.0
        sums_ref[...] = total + jnp.where(step == steps, before, sums_ref[...])
        if ending:
            _, tail_ref, _, parcel_ref = ends

            @pl.when(step == pl.num_programs(0) - 1)
            def _():
                own = sums_ref.shape[0] // parcel_ref.shape[0]
                for owner in range(parcel_ref.shape[0]):
                    parcel_ref[owner, :own] = sums_ref[owner * own : (owner + 1) * own, :]
                    parcel_ref[owner, own:] = tail_ref[owner]


def stacked(section):
    high, low = table_halves(section)
    return jnp.concatenate([high, high, low], axis=1)


def synth(me, base, slab, weight, extra, turns, tables, section, rows, hits, blocks, ending=()):
    pieces = len(slab)
    lines, dets, side = pieces * slab[0].shape[0], *slab[0].shape[1:]
    tiles = rows.size // dets
    count = math.gcd(lines // 2, UNITS)
    steps, groups = lines // (2 * count), dets // ROWS
    first = 0
    if pieces > 1 and steps > 1:
        first = pieces // steps * (steps - 1)
        ending = (early(me, base, slab[:first], weight, turns, tables, count, lines), *ending)
        slab, pieces, steps = slab[first:], pieces - first, 1
    room = (count + (base == 0)) * dets
    whole = lambda a: pl.BlockSpec(a.shape, lambda i: (0,) * a.ndim)
    later = lambda i: jnp.maximum(i - steps, 0)
    line = pl.BlockSpec((1, 1, ROWS * tiles), lambda i: (later(i), 0, 0))
    weight = pltpu.with_memory_space_constraint(weight, pltpu.HBM)
    others = [extra, turns, tables, section]
    if pieces == 1 and not first:
        slab = [pltpu.with_memory_space_constraint(slab[0], pltpu.HBM)]
        z_specs = [pl.BlockSpec((2 * count, dets, side), lambda i: (jnp.minimum(i, steps - 1), 0, 0))]
        w_spec = pl.BlockSpec((count, dets, side), lambda i: (base // count + jnp.minimum(i, steps - 1), 0, 0))
    else:
        z_specs = [whole(piece) for piece in slab]
        w_spec = pl.BlockSpec((lines // 2, dets, side), lambda i: (2 * base // lines, 0, 0))
    operands = [me, *slab, weight, *others, rows.reshape(groups, 1, -1), hits.reshape(groups, 1, -1), *ending]
    in_specs = [
        SCALAR,
        *z_specs,
        w_spec,
        *[whole(a) for a in others],
        line,
        line,
        *[whole(a) for a in ending],
    ]
    if ending:
        tail = ending[-1]
        parcel = (tail.shape[0], blocks // tail.shape[0] + tail.shape[1], tail.shape[2])
        out = [jax.ShapeDtypeStruct((groups, lines * ROWS, side), F32), jax.ShapeDtypeStruct(parcel, F32)]
        out_specs = [pl.BlockSpec((1, lines * ROWS, side), lambda i: (later(i), 0, 0)), whole(out[1])]
    else:
        out = [jax.ShapeDtypeStruct((dets * side, side), F32), jax.ShapeDtypeStruct((blocks, 2 * side), F32)]
        out_specs = [pl.BlockSpec((ROWS * side, side), lambda i: (later(i), 0)), whole(out[1])]
    return pl.pallas_call(
        functools.partial(synth_kernel, base, count, steps, first, pieces),
        grid=(steps + groups,),
        in_specs=in_specs,
        out_specs=out_specs,
        out_shape=out,
        scratch_shapes=[
            *[pltpu.VMEM((room, 2 * side), BF16)] * 2,
            pltpu.VMEM((room, 2 * side), F32),
            pltpu.VMEM((groups, lines * ROWS, side), F32),
            *[pltpu.VMEM((ROWS * tiles, 2 * side), BF16)] * 2,
            pltpu.VMEM((blocks, 2 * side), F32),
            pltpu.VMEM((ROWS * side, side), F32),
        ],
        compiler_params=LIMIT,
        cost_estimate=cost(8, lines // 2 * dets, 2 * side, 2 * side, *slab, *slab, out[0]),
        name="synth",
    )(*operands)


def emit_kernel(before_ref, held_ref, section_ref, out_ref, lined):
    side = before_ref.shape[1]
    rows = held_ref.shape[1] // ROWS
    for d in range(0, ROWS, 2):
        lines = section_lines(held_ref.at[0], section_ref, d, rows)
        for e in (0, 1):
            at = (d + e) * side
            line = lines[:, e * side : (e + 1) * side] + before_ref[at : at + side, :]
            lined[pl.ds(d + e, side, stride=ROWS), :] = line
    for n in range(side):
        out_ref[:, n * side : (n + 1) * side] = lined[n * ROWS : (n + 1) * ROWS, :]


def emit(before, held, section):
    groups, lines, side = held.shape
    out = jax.ShapeDtypeStruct((groups * ROWS, side * side), F32)
    return pl.pallas_call(
        emit_kernel,
        grid=(groups,),
        in_specs=[
            pl.BlockSpec((ROWS * side, side), lambda i: (i, 0)),
            pl.BlockSpec((1, lines, side), lambda i: (i, 0, 0)),
            pl.BlockSpec(section.shape, lambda i: (0, 0)),
        ],
        out_specs=pl.BlockSpec((ROWS, side * side), lambda i: (i, 0)),
        out_shape=out,
        scratch_shapes=[pltpu.VMEM((ROWS * side, side), F32)],
        compiler_params=LIMIT,
        cost_estimate=cost(1, side, lines // ROWS, ROWS * groups * side, before, held, out),
        name="emit",
    )(pltpu.with_memory_space_constraint(before, pltpu.HBM), held, section)


def shards(size, timestream, gains, mode_pattern, mode_weights, noise_weight, block_ids, hits, sky_rows):
    _, dets, samples = timestream.shape
    side = math.isqrt(samples)
    units = side // 2
    blocks = sky_rows.shape[0]
    half = size // 2
    quarter = size // 4
    groups = [list(range(half)), [*range(half + quarter, size), *range(half, half + quarter)]]
    opposite = [*zip(groups[0], groups[1]), *zip(groups[1], groups[0])]
    mine = lax.axis_index("det") // half

    position = (lax.axis_index("det") % half + mine * quarter) % half
    me = position.reshape(1)

    scale = jnp.broadcast_to(1.0 / gains.reshape(dets, 1), (dets, side))
    share, each = side // 2, units // size
    number = lax.iota(jnp.int32, units // 2)
    table = section_table(side, lax.iota(jnp.int32, units))
    stacks = [stacked(part.T / samples) for part in (table[:share], table[share:])]
    parts = [section_table(side, (position ^ (number // each)) * each + number % each), table[share:]]
    z = []
    for part in parts:
        z += sections(timestream.reshape(dets, samples), scale, part, [share])

    def ordered(modes):
        modes = modes.reshape(size, dets, -1)
        at = [mine * half + (mine * quarter + (position ^ k)) % half for k in range(half)]
        return jnp.concatenate([lax.dynamic_index_in_dim(modes, i, 0, keepdims=False) for i in at], axis=0)

    weights = table_halves(ordered(mode_weights).T)
    pattern = table_halves(ordered(mode_pattern))
    w = jnp.transpose(noise_weight.reshape(dets, side, side), (2, 0, 1))
    mirror = w[:units:-1, :, ::-1]
    weight = jnp.concatenate([w[:1], w[1:units] + mirror], axis=0)
    extra = w[units]
    forward, backward = inner_tables(side)
    tables = jnp.concatenate([*table_halves(forward), *table_halves(backward)], axis=0)
    turns = jnp.concatenate(twiddles(side), axis=1)

    ids_flat = block_ids.reshape(-1)
    ladder = lax.broadcasted_iota(jnp.int32, (blocks, ids_flat.shape[0]), 0)
    rows = jnp.sum(jnp.where(ids_flat[None, :] == ladder, sky_rows[:, None], 0), axis=0)
    hit = hits.reshape(-1).astype(F32)
    counts = jnp.sum(jnp.where(rows[None, :] == ladder, hit[None, :], 0.0), axis=1)

    own = blocks // size
    tail = jnp.pad(counts.reshape(size, 1, own), ((0, 0), (0, ROWS - 1), (0, 2 * side - own)))

    last = [None]

    def exchange(value):
        if last[0] is not None:
            value, _ = lax.optimization_barrier((value, last[0]))
        last[0] = lax.all_to_all(value, "det", split_axis=0, concat_axis=0, axis_index_groups=groups, tiled=True)
        return last[0]

    reverse = lambda k: sum((half >> 1 >> bit) for bit in range(half.bit_length() - 1) if k >> bit & 1)

    def trade(pieces):
        found = list(pieces)
        for k in map(reverse, range(1, half)):
            pairs = [(group[p], group[p ^ k]) for group in groups for p in range(half)]
            found[k] = lax.ppermute(pieces[k], "det", pairs)
        return found

    slabs, coeffs, others = [], [], []
    for c in (0, 1):
        if c == 0:
            slab = trade([z[0][2 * each * k : 2 * each * (k + 1)] for k in range(half)])
            last[0] = slab[half - 1]
        else:
            slab = [exchange(z[1]).reshape(half, 2 * each, dets, side)]
        slabs.append(slab)
        coeffs.append(coefficients(me, slab, weights))
        others.append(lax.ppermute(coeffs[c], "det", opposite))
    for c in (0, 1):
        slab = corrected(me, slabs[c], [coeffs[c], others[c]], pattern, apart=c == 1)
        if c == 0:
            back = [exchange(slab[0].reshape(share, dets, side))]
        else:
            slab, _ = lax.optimization_barrier((slab, last[0]))
            back = trade(slab)
        operands = [me, c * units // 2, back, weight, extra, turns, tables, stacks[c], rows, hit, blocks]
        if c == 0:
            lines, sums = synth(*operands)
        else:
            held, parcel = synth(*operands, ending=(sums, tail))

    parcel = lax.all_to_all(parcel, "det", split_axis=0, concat_axis=0, tiled=True)
    filtered = emit(lines, held, stacks[1])
    parcel = jnp.sum(parcel, axis=0)
    sky_map = parcel[:own] / jnp.sqrt(1.0 + parcel[own, :own])[:, None]
    return filtered.reshape(timestream.shape), sky_map


def solution(mesh):
    in_specs = (
        P("grp", "det", None),
        P("grp", "det"),
        P("grp", None),
        P("grp", None),
        P(("grp", "det"), None),
        P("grp", "det", None),
        P("grp", "det", None),
        P("grp"),
    )
    out_specs = (P("grp", "det", None), P(("grp", "det"), None))
    body = functools.partial(shards, mesh.shape["det"])

    return jax.shard_map(body, mesh=mesh, in_specs=in_specs, out_specs=out_specs, check_vma=False)
```

```python
import functools
import math

import jax
import jax.numpy as jnp
from jax import lax
from jax.experimental import pallas as pl
from jax.experimental.pallas import tpu as pltpu
from jax.sharding import PartitionSpec as P


F32, BF16 = jnp.float32, jnp.bfloat16
ROWS = 8
UNITS = 8
ALL = pltpu.CompilerParams(vmem_limit_bytes=60 << 20)
LIMIT = pltpu.CompilerParams(vmem_limit_bytes=16 << 20)


def halves(value):
    high = value.astype(BF16)
    return high, (value - high.astype(F32)).astype(BF16)


def table_halves(table):
    high = lax.reduce_precision(table, exponent_bits=8, mantissa_bits=7)
    return high.astype(BF16), (table - high).astype(BF16)


def mm(a, b):
    return jnp.dot(a, b, preferred_element_type=F32)


def mm3(a_pair, b_pair):
    return mm(a_pair[0], b_pair[0]) + (mm(a_pair[1], b_pair[0]) + mm(a_pair[0], b_pair[1]))


def angles(count, first, second):
    return (first * second % count).astype(F32) * (2.0 * math.pi / count)


def section_table(side, unit_of_slot):
    unit = unit_of_slot[:, None, None]
    sample = lax.broadcasted_iota(jnp.int32, (1, 1, side), 2)
    part = lax.broadcasted_iota(jnp.int32, (1, 2, 1), 1)
    nyquist = (unit == 0) & (part == 1)
    angle = angles(side, jnp.where(nyquist, side // 2, unit), sample)
    table = jnp.where((part == 0) | nyquist, jnp.cos(angle), -jnp.sin(angle))
    return table.reshape(-1, side)


def inner_tables(side):
    first = lax.broadcasted_iota(jnp.int32, (side, side), 0)
    second = lax.broadcasted_iota(jnp.int32, (side, side), 1)
    angle = angles(side, first, second)
    cos, sin = jnp.cos(angle), jnp.sin(angle)
    forward = jnp.concatenate([jnp.concatenate([cos, -sin], 1), jnp.concatenate([sin, cos], 1)], 0)
    backward = jnp.concatenate([jnp.concatenate([cos, sin], 1), jnp.concatenate([-sin, cos], 1)], 0)
    return forward, backward


def twiddles(side):
    unit = lax.broadcasted_iota(jnp.int32, (side // 2 + 8, side), 0)
    sample = lax.broadcasted_iota(jnp.int32, (side // 2 + 8, side), 1)
    angle = angles(side * side, unit, sample)
    return jnp.cos(angle), jnp.sin(angle)


def section_kernel(side, x_ref, scale_ref, high_ref, low_ref, *refs):
    out_refs, (rows, turned) = refs[:-2], refs[-2:]
    scale = scale_ref[...]
    for n in range(side):
        rows[n * ROWS : (n + 1) * ROWS, :] = x_ref[:, n * side : (n + 1) * side] * scale
    table = (high_ref[...], low_ref[...])
    for d in range(0, ROWS, 2):
        pair = jnp.concatenate([rows[pl.ds(d, side, stride=ROWS), :], rows[pl.ds(d + 1, side, stride=ROWS), :]], axis=1)
        result = mm3(table, halves(pair))
        turned[pl.ds(d, len(result), stride=ROWS), :] = result[:, :side]
        turned[pl.ds(d + 1, len(result), stride=ROWS), :] = result[:, side:]
    lines = [(out_ref, row) for out_ref in out_refs for row in range(out_ref.shape[0])]
    for k, (out_ref, row) in enumerate(lines):
        out_ref[row] = turned[k * ROWS : (k + 1) * ROWS, :]


def sections(signal, scale, table, shares):
    dets, samples = signal.shape
    side = table.shape[1]
    high, low = table_halves(table)
    whole = pl.BlockSpec(table.shape, lambda i: (0, 0))
    return pl.pallas_call(
        functools.partial(section_kernel, side),
        grid=(dets // ROWS,),
        in_specs=[pl.BlockSpec((ROWS, samples), lambda i: (i, 0)), pl.BlockSpec((ROWS, side), lambda i: (i, 0)), whole, whole],
        out_specs=[pl.BlockSpec((share, ROWS, side), lambda i: (0, i, 0)) for share in shares],
        out_shape=[jax.ShapeDtypeStruct((share, dets, side), F32) for share in shares],
        scratch_shapes=[pltpu.VMEM((side * ROWS, side), F32), pltpu.VMEM((sum(shares) * ROWS, side), F32)],
        compiler_params=LIMIT,
        name="sections",
    )(signal, scale, high, low)


def cost(passes, rows, depth, columns, *arrays):
    moved = sum(array.size * array.dtype.itemsize for array in arrays)
    return pl.CostEstimate(flops=2 * passes * rows * depth * columns, bytes_accessed=moved, transcendentals=0)


def block_reader(me_ref, z_refs):
    if len(z_refs) > 1:
        return lambda b, k: z_refs[b][k]
    return lambda b, k: z_refs[0][me_ref[0] ^ b, k]


def slab_specs(slab, step):
    if len(slab) > 1:
        return [pl.BlockSpec((step,) + piece.shape[1:], lambda i: (i, 0, 0)) for piece in slab]
    blocks, _, dets, side = slab[0].shape
    return [pl.BlockSpec((blocks, step, dets, side), lambda i: (0, i, 0, 0))]


def coeff_kernel(blocks, me_ref, *refs):
    *z_refs, high_ref, low_ref, out_ref, z_high, z_low = refs
    rows, dets, side = z_refs[0].shape[-3:]
    block = block_reader(me_ref, z_refs)
    for b in range(blocks):
        for k in range(rows):
            high, low = halves(block(b, k))
            z_high[b * dets : (b + 1) * dets, k * side : (k + 1) * side] = high
            z_low[b * dets : (b + 1) * dets, k * side : (k + 1) * side] = low
    total = mm3((high_ref[...], low_ref[...]), (z_high[...], z_low[...]))
    for k in range(rows):
        out_ref[k] = total[:, k * side : (k + 1) * side]


SCALAR = pl.BlockSpec(memory_space=pltpu.SMEM)


def coefficients(me, slab, weights):
    rows, dets, side = slab[0].shape[-3:]
    rank, depth = weights[0].shape
    out = jax.ShapeDtypeStruct((rows, rank, side), F32)
    step = math.gcd(8, rows)
    whole = pl.BlockSpec((rank, depth), lambda i: (0, 0))
    return pl.pallas_call(
        functools.partial(coeff_kernel, depth // dets),
        grid=(rows // step,),
        in_specs=[SCALAR] + slab_specs(slab, step) + [whole, whole],
        out_specs=pl.BlockSpec((step, rank, side), lambda i: (i, 0, 0)),
        out_shape=out,
        scratch_shapes=[pltpu.VMEM((depth, step * side), BF16)] * 2,
        compiler_params=LIMIT,
        cost_estimate=cost(3, rank, depth, rows * side, out, *slab),
        name="coefficients",
    )(me, *slab, *weights)


def correct_kernel(pieces, terms, me_ref, *refs):
    z_refs, c_refs = refs[:pieces], refs[pieces : pieces + terms]
    high_ref, low_ref, *out_refs = refs[pieces + terms :]
    rows, dets, side = z_refs[0].shape[-3:]
    block = block_reader(me_ref, z_refs)
    coeff = halves(jnp.concatenate([sum(c_ref[k] for c_ref in c_refs) for k in range(rows)], axis=1))
    share = mm3((high_ref[...], low_ref[...]), coeff)
    for b in range(share.shape[0] // dets):
        for k in range(rows):
            value = block(b, k) - share[b * dets : (b + 1) * dets, k * side : (k + 1) * side]
            if len(out_refs) > 1:
                out_refs[b][k] = value
            else:
                out_refs[0][me_ref[0] ^ b, k] = value


def corrected(me, slab, coeffs, pattern, apart):
    rows, dets, side = slab[0].shape[-3:]
    depth, rank = pattern[0].shape
    blocks = depth // dets
    step = math.gcd(4, rows)
    whole = pl.BlockSpec((depth, rank), lambda i: (0, 0))
    if apart:
        out = [jax.ShapeDtypeStruct((rows, dets, side), F32)] * blocks
    else:
        out = [jax.ShapeDtypeStruct((blocks, rows, dets, side), F32)]
        slab = slab[:]
    return pl.pallas_call(
        functools.partial(correct_kernel, len(slab), len(coeffs)),
        grid=(rows // step,),
        in_specs=[SCALAR]
        + slab_specs(slab, step)
        + [pl.BlockSpec((step, rank, side), lambda i: (i, 0, 0)) for _ in coeffs]
        + [whole, whole],
        out_specs=slab_specs(out, step),
        out_shape=out,
        compiler_params=ALL if apart else LIMIT,
        cost_estimate=cost(3, rank, depth, rows * side, *slab, *out, *coeffs),
        name="corrected",
    )(me, *[pltpu.with_memory_space_constraint(a, pltpu.HBM) for a in slab], *coeffs, *pattern)


def section_lines(group, section_ref, d, rows):
    pair = [group[pl.ds(d + e, rows, stride=ROWS), :] for e in (0, 1)]
    high, low = halves(jnp.concatenate(pair, axis=1))
    return mm(section_ref[...], jnp.concatenate([high, low, high], axis=0))


def unit_filter(base, count, single, w_ref, extra_ref, turn_ref, tables_ref, t_high, t_low, result, held):
    dets, side = w_ref.shape[-2:]
    has_zero = base == 0

    def turn(unit):
        pair = turn_ref[pl.ds(unit, 1), :]
        return pair[:, :side], pair[:, side:]

    def put(slot, real, imag):
        for part, value in ((0, real), (1, imag)):
            high, low = halves(value)
            t_high[slot * dets : (slot + 1) * dets, part * side : (part + 1) * side] = high
            t_low[slot * dets : (slot + 1) * dets, part * side : (part + 1) * side] = low

    def transform(high, low):
        table = lambda i: tables_ref[i * 2 * side : (i + 1) * 2 * side, :]
        middle = result.shape[0] // 2 // 16 * 16
        for at in (slice(0, middle), slice(middle, result.shape[0])):
            result[at] = mm3((t_high[at], t_low[at]), (table(high), table(low)))

    def weigh(units, read):
        half_cos, half_sin = turn(side // 2)
        turns = [turn(base + unit) for unit in units]
        for i in range(count):
            real, imag = read(i)
            if has_zero and i == 0:
                put(count, imag * half_cos, -imag * half_sin)
                imag = jnp.where(units[0] == 0, 0.0, imag)
            cos, sin = turns[i]
            put(i, real * cos + imag * sin, imag * cos - real * sin)
        transform(0, 1)
        for i in range(count + has_zero):
            weight = extra_ref[...] if i == count else w_ref[i if single else units[i]]
            at = slice(i * dets, (i + 1) * dets)
            put(i, result[at, :side] * weight, result[at, side:] * weight)
        transform(2, 3)
        for i in range(count):
            at = slice(i * dets, (i + 1) * dets)
            real, imag = result[at, :side], result[at, side:]
            cos, sin = turns[i]
            turned = imag * cos + real * sin
            if has_zero and i == 0:
                at = slice(count * dets, (count + 1) * dets)
                nyquist = result[at, :side] * half_cos - result[at, side:] * half_sin
                turned = jnp.where(units[0] == 0, nyquist, turned)
            for part, value in ((0, real * cos - imag * sin), (1, turned)):
                row = pl.multiple_of((2 * units[i] + part) * ROWS, ROWS)
                for group in range(dets // ROWS):
                    held[group, pl.ds(row, ROWS), :] = value[group * ROWS : (group + 1) * ROWS]

    return weigh


def weigh_pieces(weigh, me_ref, z_refs, first, count, steps):
    step = pl.program_id(0)
    each = z_refs[0].shape[0] // 2
    for at in range(steps):

        @pl.when(step == at)
        def _(at=at):
            slots = [divmod(at * count + i, each) for i in range(count)]
            weigh(
                [(me_ref[0] ^ (first + piece)) * each + unit for piece, unit in slots],
                lambda i: (z_refs[slots[i][0]][2 * slots[i][1]], z_refs[slots[i][0]][2 * slots[i][1] + 1]),
            )


def early_kernel(base, count, steps, pieces, me_ref, *refs):
    z_refs, (w_ref, turn_ref, tables_ref, out_ref, t_high, t_low, result) = refs[:pieces], refs[pieces:]
    weigh = unit_filter(base, count, False, w_ref, None, turn_ref, tables_ref, t_high, t_low, result, out_ref)
    weigh_pieces(weigh, me_ref, z_refs, 0, count, steps)


def early(me, base, pieces, weight, turns, tables, count, lines):
    _, dets, side = pieces[0].shape
    steps = len(pieces) * pieces[0].shape[0] // (2 * count)
    out = jax.ShapeDtypeStruct((dets // ROWS, lines * ROWS, side), F32)
    whole = lambda a: pl.BlockSpec(a.shape, lambda i: (0,) * a.ndim)
    return pl.pallas_call(
        functools.partial(early_kernel, base, count, steps, len(pieces)),
        grid=(steps,),
        in_specs=[SCALAR]
        + [whole(piece) for piece in pieces]
        + [pl.BlockSpec((lines // 2, dets, side), lambda i: (2 * base // lines, 0, 0)), whole(turns), whole(tables)],
        out_specs=whole(out),
        out_shape=out,
        scratch_shapes=[pltpu.VMEM((count * dets, 2 * side), BF16)] * 2 + [pltpu.VMEM((count * dets, 2 * side), F32)],
        compiler_params=LIMIT,
        cost_estimate=cost(6, steps * count * dets, 2 * side, 2 * side, out, *pieces),
        name="early",
    )(me, *pieces, weight, turns, tables)


def synth_kernel(base, count, steps, first, pieces, me_ref, *refs):
    z_refs, refs = refs[:pieces], refs[pieces:]
    w_ref, extra_ref, turn_ref, tables_ref, section_ref, rows_ref, hits_ref, *refs = refs
    *ends, t_high, t_low, result, held, tile_high, tile_low, total_ref, one = refs
    if first:
        before_ref, *ends = ends
    ending = len(ends) == 4
    _, side = z_refs[0].shape[-2:]
    step = pl.program_id(0)
    weigh = unit_filter(
        base, count, pieces == 1 and not first, w_ref, extra_ref, turn_ref, tables_ref, t_high, t_low, result, held
    )
    if first:

        @pl.when(step == 0)
        def _():
            held[...] = before_ref[...]

    if pieces == 1 and not first:

        @pl.when(step < steps)
        def _():
            z_ref = z_refs[0]
            weigh([step * count + i for i in range(count)], lambda i: (z_ref[2 * i], z_ref[2 * i + 1]))

    else:
        weigh_pieces(weigh, me_ref, z_refs, first, count, steps)

    @pl.when(step >= steps)
    def _():
        rows = held.shape[1] // ROWS
        tiles = tile_high.shape[0] // ROWS
        group = held.at[step - steps]
        lines_ref = one if ending else ends[0]
        for d in range(0, ROWS, 2):
            lines = section_lines(group, section_ref, d, rows)
            for e in (0, 1):
                at = (d + e) * side
                lines_ref[at : at + side, :] = lines[:, e * side : (e + 1) * side]
                for half in (0, 1):
                    high, low = halves(lines_ref[pl.ds(at + half, side // 2, stride=2), :])
                    into = slice((d + e) * tiles, (d + e + 1) * tiles)
                    tile_high[into, half * side : (half + 1) * side] = high
                    tile_low[into, half * side : (half + 1) * side] = low
        if ending:
            ends[2][0] = group[...]
        sums_ref = total_ref if ending else ends[1]
        ladder = lax.broadcasted_iota(jnp.int32, (sums_ref.shape[0], ROWS * tiles), 0)
        chosen = jnp.where(rows_ref[0] == ladder, hits_ref[0], 0.0).astype(BF16)
        total = mm(chosen, tile_high[...]) + mm(chosen, tile_low[...])
        before = ends[0][...] if ending else 0.0
        sums_ref[...] = total + jnp.where(step == steps, before, sums_ref[...])
        if ending:
            _, tail_ref, _, parcel_ref = ends

            @pl.when(step == pl.num_programs(0) - 1)
            def _():
                own = sums_ref.shape[0] // parcel_ref.shape[0]
                for owner in range(parcel_ref.shape[0]):
                    parcel_ref[owner, :own] = sums_ref[owner * own : (owner + 1) * own, :]
                    parcel_ref[owner, own:] = tail_ref[owner]


def stacked(section):
    high, low = table_halves(section)
    return jnp.concatenate([high, high, low], axis=1)


def synth(me, base, slab, weight, extra, turns, tables, section, rows, hits, blocks, ending=()):
    pieces = len(slab)
    lines, dets, side = pieces * slab[0].shape[0], *slab[0].shape[1:]
    tiles = rows.size // dets
    count = math.gcd(lines // 2, UNITS)
    steps, groups = lines // (2 * count), dets // ROWS
    first = 0
    if pieces > 1 and steps > 1:
        first = pieces // steps * (steps - 1)
        ending = (early(me, base, slab[:first], weight, turns, tables, count, lines), *ending)
        slab, pieces, steps = slab[first:], pieces - first, 1
    room = (count + (base == 0)) * dets
    whole = lambda a: pl.BlockSpec(a.shape, lambda i: (0,) * a.ndim)
    later = lambda i: jnp.maximum(i - steps, 0)
    line = pl.BlockSpec((1, 1, ROWS * tiles), lambda i: (later(i), 0, 0))
    weight = pltpu.with_memory_space_constraint(weight, pltpu.HBM)
    others = [extra, turns, tables, section]
    if pieces == 1 and not first:
        slab = [pltpu.with_memory_space_constraint(slab[0], pltpu.HBM)]
        z_specs = [pl.BlockSpec((2 * count, dets, side), lambda i: (jnp.minimum(i, steps - 1), 0, 0))]
        w_spec = pl.BlockSpec((count, dets, side), lambda i: (base // count + jnp.minimum(i, steps - 1), 0, 0))
    else:
        z_specs = [whole(piece) for piece in slab]
        w_spec = pl.BlockSpec((lines // 2, dets, side), lambda i: (2 * base // lines, 0, 0))
    operands = [me, *slab, weight, *others, rows.reshape(groups, 1, -1), hits.reshape(groups, 1, -1), *ending]
    in_specs = [
        SCALAR,
        *z_specs,
        w_spec,
        *[whole(a) for a in others],
        line,
        line,
        *[whole(a) for a in ending],
    ]
    if ending:
        tail = ending[-1]
        parcel = (tail.shape[0], blocks // tail.shape[0] + tail.shape[1], tail.shape[2])
        out = [jax.ShapeDtypeStruct((groups, lines * ROWS, side), F32), jax.ShapeDtypeStruct(parcel, F32)]
        out_specs = [pl.BlockSpec((1, lines * ROWS, side), lambda i: (later(i), 0, 0)), whole(out[1])]
    else:
        out = [jax.ShapeDtypeStruct((dets * side, side), F32), jax.ShapeDtypeStruct((blocks, 2 * side), F32)]
        out_specs = [pl.BlockSpec((ROWS * side, side), lambda i: (later(i), 0)), whole(out[1])]
    return pl.pallas_call(
        functools.partial(synth_kernel, base, count, steps, first, pieces),
        grid=(steps + groups,),
        in_specs=in_specs,
        out_specs=out_specs,
        out_shape=out,
        scratch_shapes=[
            *[pltpu.VMEM((room, 2 * side), BF16)] * 2,
            pltpu.VMEM((room, 2 * side), F32),
            pltpu.VMEM((groups, lines * ROWS, side), F32),
            *[pltpu.VMEM((ROWS * tiles, 2 * side), BF16)] * 2,
            pltpu.VMEM((blocks, 2 * side), F32),
            pltpu.VMEM((ROWS * side, side), F32),
        ],
        compiler_params=LIMIT,
        cost_estimate=cost(8, lines // 2 * dets, 2 * side, 2 * side, *slab, *slab, out[0]),
        name="synth",
    )(*operands)


def emit_kernel(before_ref, held_ref, section_ref, out_ref, lined):
    side = before_ref.shape[1]
    rows = held_ref.shape[1] // ROWS
    for d in range(0, ROWS, 2):
        lines = section_lines(held_ref.at[0], section_ref, d, rows)
        for e in (0, 1):
            at = (d + e) * side
            line = lines[:, e * side : (e + 1) * side] + before_ref[at : at + side, :]
            lined[pl.ds(d + e, side, stride=ROWS), :] = line
    for n in range(side):
        out_ref[:, n * side : (n + 1) * side] = lined[n * ROWS : (n + 1) * ROWS, :]


def emit(before, held, section):
    groups, lines, side = held.shape
    out = jax.ShapeDtypeStruct((groups * ROWS, side * side), F32)
    return pl.pallas_call(
        emit_kernel,
        grid=(groups,),
        in_specs=[
            pl.BlockSpec((ROWS * side, side), lambda i: (i, 0)),
            pl.BlockSpec((1, lines, side), lambda i: (i, 0, 0)),
            pl.BlockSpec(section.shape, lambda i: (0, 0)),
        ],
        out_specs=pl.BlockSpec((ROWS, side * side), lambda i: (i, 0)),
        out_shape=out,
        scratch_shapes=[pltpu.VMEM((ROWS * side, side), F32)],
        compiler_params=LIMIT,
        cost_estimate=cost(1, side, lines // ROWS, ROWS * groups * side, before, held, out),
        name="emit",
    )(pltpu.with_memory_space_constraint(before, pltpu.HBM), held, section)


def shards(size, timestream, gains, mode_pattern, mode_weights, noise_weight, block_ids, hits, sky_rows):
    _, dets, samples = timestream.shape
    side = math.isqrt(samples)
    units = side // 2
    blocks = sky_rows.shape[0]
    half = size // 2
    quarter = size // 4
    groups = [list(range(half)), [*range(half + quarter, size), *range(half, half + quarter)]]
    opposite = [*zip(groups[0], groups[1]), *zip(groups[1], groups[0])]
    mine = lax.axis_index("det") // half

    position = (lax.axis_index("det") % half + mine * quarter) % half
    me = position.reshape(1)

    scale = jnp.broadcast_to(1.0 / gains.reshape(dets, 1), (dets, side))
    share, each = side // 2, units // size
    number = lax.iota(jnp.int32, units // 2)
    table = section_table(side, lax.iota(jnp.int32, units))
    stacks = [stacked(part.T / samples) for part in (table[:share], table[share:])]
    parts = [section_table(side, (position ^ (number // each)) * each + number % each), table[share:]]
    z = []
    for c, part in enumerate(parts):
        signal = timestream.reshape(dets, samples)
        signal = pltpu.with_memory_space_constraint(signal, pltpu.HBM) if c else signal
        z += sections(signal, scale, part, [share])

    def ordered(modes):
        modes = modes.reshape(size, dets, -1)
        at = [mine * half + (mine * quarter + (position ^ k)) % half for k in range(half)]
        return jnp.concatenate([lax.dynamic_index_in_dim(modes, i, 0, keepdims=False) for i in at], axis=0)

    weights = table_halves(ordered(mode_weights).T)
    pattern = table_halves(ordered(mode_pattern))
    w = jnp.transpose(noise_weight.reshape(dets, side, side), (2, 0, 1))
    mirror = w[:units:-1, :, ::-1]
    weight = jnp.concatenate([w[:1], w[1:units] + mirror], axis=0)
    extra = w[units]
    forward, backward = inner_tables(side)
    tables = jnp.concatenate([*table_halves(forward), *table_halves(backward)], axis=0)
    turns = jnp.concatenate(twiddles(side), axis=1)

    ids_flat = block_ids.reshape(-1)
    ladder = lax.broadcasted_iota(jnp.int32, (blocks, ids_flat.shape[0]), 0)
    rows = jnp.sum(jnp.where(ids_flat[None, :] == ladder, sky_rows[:, None], 0), axis=0)
    hit = hits.reshape(-1).astype(F32)
    counts = jnp.sum(jnp.where(rows[None, :] == ladder, hit[None, :], 0.0), axis=1)

    own = blocks // size
    tail = jnp.pad(counts.reshape(size, 1, own), ((0, 0), (0, ROWS - 1), (0, 2 * side - own)))

    last = [None]

    def exchange(value):
        if last[0] is not None:
            value, _ = lax.optimization_barrier((value, last[0]))
        last[0] = lax.all_to_all(value, "det", split_axis=0, concat_axis=0, axis_index_groups=groups, tiled=True)
        return last[0]

    reverse = lambda k: sum((half >> 1 >> bit) for bit in range(half.bit_length() - 1) if k >> bit & 1)

    def trade(pieces):
        found = list(pieces)
        for k in map(reverse, range(1, half)):
            pairs = [(group[p], group[p ^ k]) for group in groups for p in range(half)]
            found[k] = lax.ppermute(pieces[k], "det", pairs)
        return found

    slabs, coeffs, others = [], [], []
    for c in (0, 1):
        if c == 0:
            slab = trade([z[0][2 * each * k : 2 * each * (k + 1)] for k in range(half)])
            last[0] = slab[half - 1]
        else:
            slab = [exchange(z[1]).reshape(half, 2 * each, dets, side)]
        slabs.append(slab)
        coeffs.append(coefficients(me, slab, weights))
        others.append(lax.ppermute(coeffs[c], "det", opposite))
    for c in (0, 1):
        slab = corrected(me, slabs[c], [coeffs[c], others[c]], pattern, apart=c == 1)
        if c == 0:
            back = [exchange(slab[0].reshape(share, dets, side))]
        else:
            slab, _ = lax.optimization_barrier((slab, last[0]))
            back = trade(slab)
        operands = [me, c * units // 2, back, weight, extra, turns, tables, stacks[c], rows, hit, blocks]
        if c == 0:
            lines, sums = synth(*operands)
        else:
            held, parcel = synth(*operands, ending=(sums, tail))

    parcel = lax.all_to_all(parcel, "det", split_axis=0, concat_axis=0, tiled=True)
    filtered = emit(lines, held, stacks[1])
    parcel = jnp.sum(parcel, axis=0)
    sky_map = parcel[:own] / jnp.sqrt(1.0 + parcel[own, :own])[:, None]
    return filtered.reshape(timestream.shape), sky_map


def solution(mesh):
    in_specs = (
        P("grp", "det", None),
        P("grp", "det"),
        P("grp", None),
        P("grp", None),
        P(("grp", "det"), None),
        P("grp", "det", None),
        P("grp", "det", None),
        P("grp"),
    )
    out_specs = (P("grp", "det", None), P(("grp", "det"), None))
    body = functools.partial(shards, mesh.shape["det"])

    return jax.shard_map(body, mesh=mesh, in_specs=in_specs, out_specs=out_specs, check_vma=False)
```
